512 devices in a mesh: atoms: 64 (over x, z, core), width: 8 (over y).
Axes of the slice: x: 4, y: 8, z: 8, core: 2. Of those that a mesh axis runs over, the one named last changes fastest.
Arguments:
- tokens: bfloat16 [8192, 8192], P('atoms', 'width'), may hold values from -6 to 6
- dec_bias: float32 [8192], P('width'), may hold values from -3 to 3
- encoder: bfloat16 [8192, 8192], P('atoms', 'width'), may hold values from -1.5 to 1.5
- enc_bias: float32 [8192], P('atoms'), may hold values from -24 to 24
- decoder: bfloat16 [8192, 8192], P('atoms', 'width'), may hold values from -0.25 to 0.25
- atom_ids: int32 [8192, 16], P('atoms'), may hold values from 0 to 8191, as said below
- block_count: int32 [64], P('atoms'), may hold values from 1 to 2, as said below
Outputs:
- residual: bfloat16 [8192, 8192], P('atoms', 'width')
- encoder_grad: bfloat16 [8192, 8192], P('atoms', 'width')
- decoder_grad: bfloat16 [8192, 8192], P('atoms', 'width')
- bias_grad: float32 [8192], P('atoms')
The draws below stay inside these ranges and needn't reach their ends.
Inputs may be any that keep to these rules, and one draw needn't show every extreme that they name: atom_ids[t, 2g] and atom_ids[t, 2g + 1] are two different atom slots of one owner o (slot // 128 = o), both below o * 128 + 64 block_count[o]; the 8 owners of one token differ. Of the 128 tokens of one index of atoms, at most 24 use any one owner, and in every draw some owner is used by exactly 24 tokens of every index of atoms. `block_count`: every draw has an owner with 2 live blocks and one with a single live block.
All inputs are finite; a program needn't handle non-finite values.
Results may differ from the reference program's by a relative error of at most 0.018.
Values may be sent and summed in bfloat16 or wider, within the bound.
No kernel may reach another device: no remote copies, remote signals or barrier semaphores. Data moves between devices by JAX's collectives and lax.ppermute only.
A program may use at most 64 MiB of HBM per device.

```python
import math
import jax
import jax.numpy as jnp
from jax import lax

D = 8192
GROUPS = 8
BLOCK = 64
BLK_DEV = 2
ATOMS = 8192
TOK_DEV = 128
TOKENS = 8192
N_ATOMS = 64


def routing(key):
    base_key = jax.random.fold_in(key, 5)
    k_hot, k_count, k_full, k_low, k_src = jax.random.split(base_key, 5)
    all_owners = jnp.arange(N_ATOMS)
    counts = jax.random.randint(k_count, (N_ATOMS,), 1, BLK_DEV + 1)
    full_owner = jax.random.randint(k_full, (), 0, N_ATOMS)
    low_owner = (full_owner + jax.random.randint(k_low, (), 1, N_ATOMS)) % N_ATOMS
    counts = jnp.where(all_owners == full_owner, BLK_DEV, jnp.where(all_owners == low_owner, 1, counts))
    hot_owner = jax.random.randint(k_hot, (), 0, N_ATOMS)
    residues = N_ATOMS // GROUPS
    capacity = 3 * TOK_DEV * GROUPS // (2 * N_ATOMS)

    def one_source(source_key):
        k_perm, k_tok, k_first, k_shift = jax.random.split(source_key, 4)
        owner_order = jax.random.permutation(k_perm, N_ATOMS)
        hot_place = jnp.sum(jnp.where(owner_order == hot_owner, all_owners, 0))
        hot_res = hot_place % residues
        token_rank = jax.random.permutation(k_tok, TOK_DEV)
        other_res = (hot_res + 1 + (token_rank - capacity) % max(residues - 1, 1)) % residues
        residue = jnp.where(token_rank < capacity, hot_res, other_res)
        pick_index = residue[:, None] + residues * jnp.arange(GROUPS)[None, :]
        owner_of = owner_order[pick_index]
        live_atoms = counts[owner_of] * BLOCK
        first_atom = jax.random.randint(k_first, (TOK_DEV, GROUPS), 0, live_atoms)
        atom_shift = jax.random.randint(k_shift, (TOK_DEV, GROUPS), 1, live_atoms)
        second_atom = (first_atom + atom_shift) % live_atoms
        base_id = owner_of * (BLK_DEV * BLOCK)
        return jnp.stack([base_id + first_atom, base_id + second_atom], axis=2).reshape(TOK_DEV, 2 * GROUPS)
    chosen = jax.vmap(one_source)(jax.random.split(k_src, N_ATOMS))
    return (chosen.reshape(N_ATOMS * TOK_DEV, 2 * GROUPS).astype(jnp.int32), counts.astype(jnp.int32))


def draw_atom_ids(key, part):
    return routing(key)[0]


def draw_block_count(key, part):
    return routing(key)[1]


def draw_decoder(key, part):
    key_noise, key_rows, key_cols = jax.random.split(jax.random.fold_in(key, 11), 3)
    noise = jnp.clip(jax.random.normal(key_noise, (ATOMS, D), jnp.float32), -6.0, 6.0)
    row_scale = jnp.exp(jax.random.uniform(key_rows, (ATOMS, 1), jnp.float32, -1.15, 1.15))
    col_scale = jnp.exp(jax.random.uniform(key_cols, (1, D), jnp.float32, -1.15, 1.15))
    values = noise * row_scale * col_scale * (0.68 / jnp.sqrt(jnp.float32(D)))
    return jnp.clip(values, -0.25, 0.25).astype(jnp.bfloat16)


def levels(stream_key, shape, pieces, smallest, top_value):
    factor_of, own = 1.0, jax.random.fold_in(stream_key, 6)
    for dim, blocks in pieces:
        draws = jnp.exp(jax.random.uniform(jax.random.fold_in(own, dim), (blocks,), jnp.float32, smallest / len(pieces), top_value / len(pieces)))
        factor_of = factor_of * jnp.repeat(draws, shape[dim] // blocks).reshape([-1 if axis == dim else 1 for axis in range(len(shape))])
    return factor_of


def gaussian(stream_key, shape, scale, limit, pieces=(), kind=jnp.bfloat16):
    result = scale * jax.random.normal(stream_key, shape, jnp.float32)
    if pieces:
        result = result * levels(stream_key, shape, pieces, -0.22, 0.18)
    return jnp.clip(result, -limit, limit).astype(kind)


def setup_inputs(seed: int = 0) -> dict:
    key_list = jax.random.split(jax.random.key(seed), 8)
    tokens = gaussian(key_list[0], (TOKENS, D), 1.0, 6.0, ((0, 64), (1, 8)))
    dec_bias = gaussian(key_list[1], (D,), 0.5, 3.0, ((0, 8),), jnp.float32)
    encoder = gaussian(key_list[2], (ATOMS, D), 16 ** -0.5, 1.5, ((0, 64), (1, 8)))
    enc_bias = gaussian(key_list[3], (ATOMS,), 4.0, 24.0, ((0, 64),), jnp.float32)
    decoder = draw_decoder(jax.random.fold_in(key_list[7], 71), 0)
    atom_ids = draw_atom_ids(jax.random.fold_in(key_list[7], 71), 0)
    block_count = draw_block_count(jax.random.fold_in(key_list[7], 71), 0)
    return {"tokens": tokens, "dec_bias": dec_bias, "encoder": encoder, "enc_bias": enc_bias, "decoder": decoder, "atom_ids": atom_ids, "block_count": block_count}


coherence = 128.0
loss_grad = 1.0 / 32.0
epsilon = 1e-06

def rounded(value):
    return lax.optimization_barrier(value.astype(jnp.bfloat16))

def coherence_grad(rows, alive):
    raw_gram = jnp.dot(rows, rows.T, preferred_element_type=jnp.float32)
    norms = jnp.sqrt(jnp.diagonal(raw_gram) + epsilon)
    norm_pair = norms[:, None] * norms[None, :]
    cosine = raw_gram / norm_pair
    extent = rows.shape[0]
    on_diagonal = jnp.arange(extent)[:, None] == jnp.arange(extent)[None, :]
    coupled = jnp.where(on_diagonal, 0.0, alive[:, None] * alive[None, :] * cosine)
    spread = lax.optimization_barrier(jnp.sum(coupled * cosine, axis=1))
    diag_term = jnp.where(on_diagonal, (spread / (norms * norms))[:, None], 0.0)
    weights = (4.0 * coherence * (coupled / norm_pair - diag_term)).astype(jnp.bfloat16)
    return jnp.dot(weights, rows, preferred_element_type=jnp.float32)

def owner_grad(pair):
    return coherence_grad(pair[0], pair[1])

def reference(tokens, dec_bias, encoder, enc_bias, decoder, atom_ids, block_count):
    total, width = tokens.shape
    pick = atom_ids.shape[1]
    atoms_total = encoder.shape[0]
    centered = (tokens.astype(jnp.float32) - dec_bias).astype(jnp.bfloat16)
    block_rows = math.gcd(total, 256)

    def step(carry, index):
        enc_acc, dec_acc, bias_acc = carry
        start = index * block_rows
        cen_rows = lax.dynamic_slice_in_dim(centered, start, block_rows, 0)
        tok_rows = lax.dynamic_slice_in_dim(tokens, start, block_rows, 0)
        chosen = lax.dynamic_slice_in_dim(atom_ids, start, block_rows, 0)
        enc_rows = encoder[chosen].astype(jnp.float32)
        pre = jnp.einsum('td,tkd->tk', cen_rows.astype(jnp.float32), enc_rows) + enc_bias[chosen]
        act = rounded(pre).astype(jnp.float32)
        dec_rows = decoder[chosen].astype(jnp.float32)
        terms = act[:, :, None] * dec_rows
        decoded = rounded(lax.optimization_barrier(jnp.sum(terms.reshape(block_rows, pick // 2, 2, width), axis=2))).astype(jnp.float32)
        resid = rounded(lax.optimization_barrier(jnp.sum(decoded, axis=1)) + dec_bias - tok_rows.astype(jnp.float32))
        resid_wide = resid.astype(jnp.float32)
        act_grad = jnp.einsum('td,tkd->tk', resid_wide, dec_rows) * loss_grad
        flat_ids = chosen.reshape(-1)
        enc_terms = (rounded(act_grad).astype(jnp.float32)[:, :, None] * cen_rows.astype(jnp.float32)[:, None, :]).reshape(-1, width)
        dec_terms = (act[:, :, None] * resid_wide[:, None, :]).reshape(-1, width)
        enc_acc = enc_acc.at[flat_ids].add(enc_terms)
        dec_acc = dec_acc.at[flat_ids].add(dec_terms)
        bias_acc = bias_acc.at[flat_ids].add(act_grad.reshape(-1))
        return ((enc_acc, dec_acc, bias_acc), resid)
    start_state = (jnp.zeros((atoms_total, width), jnp.float32), jnp.zeros((atoms_total, width), jnp.float32), jnp.zeros((atoms_total,), jnp.float32))
    (enc_acc, dec_acc, bias_acc), resid_blocks = lax.scan(step, start_state, jnp.arange(total // block_rows, dtype=jnp.int32))
    residual = resid_blocks.reshape(total, width)
    owners = block_count.shape[0]
    atom_dev = atoms_total // owners
    alive = (jnp.arange(atom_dev)[None, :] < block_count[:, None] * BLOCK).astype(jnp.float32)
    penalty = lax.map(owner_grad, (decoder.reshape(owners, atom_dev, width), alive))
    encoder_grad = enc_acc.astype(jnp.bfloat16)
    decoder_grad = (dec_acc * loss_grad + penalty.reshape(atoms_total, width)).astype(jnp.bfloat16)
    return (residual, encoder_grad, decoder_grad, bias_acc)
```

```python
import jax
import jax.numpy as jnp
from jax import lax
from jax.experimental import pallas as pl
from jax.experimental.pallas import tpu as pltpu
from jax.sharding import PartitionSpec as P

NX, NZ, NC, NY = 4, 8, 2, 8
BLOCK = 64
R = 128
COHERENCE = 128.0
LOSS_GRAD = 1.0 / 32.0
EPSILON = 1e-06
BF, F32, I32 = jnp.bfloat16, jnp.float32, jnp.int32
VMEM = 48 * 1024 * 1024


def _place(x, z, c):
    return ((x % NX) * NZ + z % NZ) * NC + c % NC


def _perm(dx=0, dz=0, dc=0):
    return [
        (_place(x, z, c), _place(x + dx, z + dz, c + dc))
        for x in range(NX)
        for z in range(NZ)
        for c in range(NC)
    ]


def move(value, **shift):
    return lax.ppermute(value, "atoms", _perm(**shift))


def call(body, outs, *args, scratch=(), specs=None, name):
    return pl.pallas_call(
        body,
        out_shape=outs,
        in_specs=specs,
        scratch_shapes=scratch,
        compiler_params=pltpu.CompilerParams(vmem_limit_bytes=VMEM),
        name=name,
    )(*args)


def sds(shape, dtype):
    return jax.ShapeDtypeStruct(shape, dtype)


def whole(n):
    return [pl.BlockSpec(memory_space=pltpu.VMEM)] * n


SMEM_SPEC = pl.BlockSpec(memory_space=pltpu.SMEM)
ANY_SPEC = pl.BlockSpec(memory_space=pl.ANY)

NT = (((1,), (1,)), ((), ()))
NN = (((1,), (0,)), ((), ()))


def dot(a, b, dims):
    return lax.dot_general(a, b, dims, preferred_element_type=F32)


def rows_iota(shape):
    return lax.broadcasted_iota(I32, shape, 0)


def lanes_iota(shape):
    return lax.broadcasted_iota(I32, shape, 1)


def center_body(tokens, dec_bias, atom_ids, out):
    out[0:R, :] = (tokens[...].astype(F32) - dec_bias[...]).astype(BF)
    ids = atom_ids[...]
    owner = (ids >> 7).astype(F32).astype(BF)
    local = (ids & 127).astype(F32).astype(BF)
    row, col = rows_iota((8, 16)), lanes_iota((8, 16))
    even = (col == 2 * row).astype(F32).astype(BF)
    odd = (col == 2 * row + 1).astype(F32).astype(BF)
    out[R : R + 8, 0:128] = dot(even, owner, NT).astype(BF)
    out[R : R + 8, 128:256] = dot(even, local, NT).astype(BF)
    out[R : R + 8, 256:384] = dot(odd, local, NT).astype(BF)
    out[R : R + 8, 384:1024] = jnp.zeros((8, 640), BF)


def pack_body(encoder, decoder, enc_bias, out, gram):
    out[0:R, :] = encoder[...]
    out[R : 2 * R, :] = decoder[...]
    bias = jnp.broadcast_to(enc_bias[...], (8, 128))
    high = bias.astype(BF)
    rest = bias - high.astype(F32)
    mid = rest.astype(BF)
    low = (rest - mid.astype(F32)).astype(BF)
    out[2 * R : 2 * R + 8, 0:128] = high
    out[2 * R : 2 * R + 8, 128:256] = mid
    out[2 * R : 2 * R + 8, 256:384] = low
    out[2 * R : 2 * R + 8, 384:1024] = jnp.zeros((8, 640), BF)
    gram[...] = dot(decoder[...], decoder[...], NT)


def locate(ext, pos):
    x, z, c = pos[0], pos[1], pos[2]
    owner = ext[:, 0:128].astype(I32)
    first, second = ext[:, 128:256].astype(I32), ext[:, 256:384].astype(I32)
    dx = (((owner >> 4) - x) + NX) & 3
    b = jnp.where(dx == 0, 0, jnp.where(dx == 3, 1, jnp.where(dx == 1, 2, 3)))
    b = b + jnp.where((owner & 1) == c, 0, 4)
    b = jnp.where(((owner >> 1) & 7) == z, b, -1)
    slot = rows_iota((8, 128))
    at_a = jnp.full((8, 128), -1, I32)
    at_b = jnp.full((8, 128), -1, I32)
    for g in range(8):
        hit = jnp.broadcast_to(b[g : g + 1, :], (8, 128)) == slot
        at_a = jnp.where(hit, jnp.broadcast_to(first[g : g + 1, :], (8, 128)), at_a)
        at_b = jnp.where(hit, jnp.broadcast_to(second[g : g + 1, :], (8, 128)), at_b)
    return at_a, at_b


def pick_into(out, tables, tok, places):
    n = len(places)
    atom = rows_iota((R, 128))
    for h, table in enumerate(tables):
        scores = dot(table[0 : 4 * R, :], tok, NT)
        for i in range(n):
            at_a, at_b = places[i]
            for q in range(4):
                b = 4 * h + q
                part = scores[q * R : (q + 1) * R, i * 128 : (i + 1) * 128]
                for s, at in ((0, at_a), (1, at_b)):
                    row = jnp.broadcast_to(at[b : b + 1, :], (R, 128))
                    got = jnp.sum(jnp.where(atom == row, part, 0.0), axis=0, keepdims=True)
                    out[16 * i + 8 * s + b : 16 * i + 8 * s + b + 1, :] = got


def score_body(split, n):
    def body(pos, own, other, *refs):
        chunks, (picks, where) = refs[:-2], refs[-2:]
        if split:
            toks = [jnp.concatenate([chunks[0][...], chunks[1][0:64, :]], axis=0)]
            exts = [chunks[1][64:72, 0:384].astype(F32)]
        else:
            toks = [c[0:R, :] for c in chunks]
            exts = [c[R : R + 8, 0:384].astype(F32) for c in chunks]
        places = [locate(ext, pos) for ext in exts]
        for i, (at_a, at_b) in enumerate(places):
            where[16 * i : 16 * i + 8, :] = at_a
            where[16 * i + 8 : 16 * i + 16, :] = at_b
        tok = toks[0] if n == 1 else jnp.concatenate(toks, axis=0)
        pick_into(picks, (own, other), tok, places)

    return body


def back_body(split, n, first):
    def body(own, other, where, *refs):
        chunks, picks = refs[:-1], refs[-1]
        toks = [c[...] for c in chunks]
        places = []
        for i in range(n):
            at = 16 * (first + i)
            places.append((where[at : at + 8, :], where[at + 8 : at + 16, :]))
        tok = toks[0] if len(toks) == 1 else jnp.concatenate(toks, axis=0)
        pick_into(picks, (own, other), tok, places)

    return body


def send_body(p0, p1, p2, p3, gram, out):
    picks = jnp.concatenate([p0[...], p1[...], p2[...], p3[...]], axis=0).astype(BF)
    high = gram[...].astype(BF)
    low = (gram[...] - high.astype(F32)).astype(BF)
    for d in range(NY):
        out[d, 0:128, :] = picks
        out[d, 128:144, :] = high[16 * d : 16 * d + 16, :]
        out[d, 144:160, :] = low[16 * d : 16 * d + 16, :]


def resend_body(p0, p1, p2, p3, rows, out):
    picks = jnp.concatenate([p0[...], p1[...], p2[...], p3[...]], axis=0).astype(BF)
    for d in range(NY):
        out[d, 0:128, :] = picks
        out[d, 128:160, :] = rows[...]


def total(got, lo, hi):
    acc = got[0, lo:hi, :].astype(F32)
    for d in range(1, NY):
        acc = acc + got[d, lo:hi, :].astype(F32)
    return acc


def table_rows(at_t, val_t, m, half):
    lane = lanes_iota((R, 128))
    parts = []
    for q in range(4):
        k = 16 * m + 4 * half + q
        first = jnp.where(lane == at_t[:, k : k + 1], val_t[:, k : k + 1], 0.0)
        second = jnp.where(lane == at_t[:, k + 8 : k + 9], val_t[:, k + 8 : k + 9], 0.0)
        parts.append((first + second).astype(BF))
    return jnp.concatenate(parts, axis=1)


def decode(at_t, val_t, own, other, ms):
    halves = []
    for half, table in enumerate((own, other)):
        rows = [table_rows(at_t, val_t, m, half) for m in ms]
        rows = rows[0] if len(ms) == 1 else jnp.concatenate(rows, axis=0)
        halves.append(dot(rows, table[0 : 4 * R, :], NN))
    return halves[0] + halves[1]


def act_body(got, own, other, w0, w1, w2, w3, act, where, at_t, act_t, gram_rows, out):
    pre = total(got, 0, 128)
    bias = []
    for table in (own, other):
        for q in range(4):
            ext = table[4 * R + 8 * q : 4 * R + 8 * q + 8, 0:384].astype(F32)
            bias.append((ext[0:1, 0:128] + ext[0:1, 128:256]) + ext[0:1, 256:384])
    bias = jnp.concatenate(bias, axis=0)
    at = jnp.concatenate([w0[...], w1[...], w2[...], w3[...]], axis=0)
    shift = [
        jnp.take_along_axis(bias, jnp.maximum(at[8 * k : 8 * k + 8, :], 0), axis=1, mode="promise_in_bounds")
        for k in range(16)
    ]
    pre = pre + jnp.concatenate(shift, axis=0)
    value = jnp.where(at >= 0, pre.astype(BF).astype(F32), 0.0)
    act[...] = value
    where[...] = at
    turned = at.astype(F32).T.astype(I32)
    value_t = value.T
    at_t[...] = turned
    act_t[...] = value_t
    rows = total(got, 128, 144) + total(got, 144, 160)
    high = rows.astype(BF)
    gram_rows[0:16, :] = high
    gram_rows[16:32, :] = (rows - high.astype(F32)).astype(BF)
    out[...] = decode(turned, value_t, own, other, (7,)).astype(BF)


def decode_body(ms):
    def body(at_t, act_t, own, other, *outs):
        got = decode(at_t[...], act_t[...], own, other, ms)
        for i, out in enumerate(outs):
            out[...] = got[i * R : (i + 1) * R, :].astype(out.dtype)

    return body


def turned_table(at, val, b):
    atom = rows_iota((R, 128))
    parts = []
    for m in range(8):
        k = 16 * m + b
        first = jnp.where(atom == at[k : k + 1, :], val[k : k + 1, :], 0.0)
        second = jnp.where(atom == at[k + 8 : k + 9, :], val[k + 8 : k + 9, :], 0.0)
        parts.append(first + second)
    return parts


def load_rows(refs, rows, sem):
    copies, at = [], 0
    for i, ref in enumerate(refs):
        n = min(ref.shape[0], R)
        if ref.shape[0] == 72:
            n = 64
        copies.append(pltpu.make_async_copy(ref.at[pl.ds(0, n)], rows.at[pl.ds(at, n)], sem.at[i]))
        at += n
    for copy in copies:
        copy.start()
    return copies


def fitted_body(at, act, *refs):
    chunks, (own, other, rows, sem) = refs[:9], refs[9:]
    copies = load_rows(chunks, rows, sem)
    tables = []
    for half in (1, 0):
        parts = []
        for q in range(4):
            parts.append(jnp.concatenate(turned_table(at, act, 4 * half + q), axis=1).astype(BF))
        tables.append(jnp.concatenate(parts, axis=0))
    for copy in copies:
        copy.wait()
    other[...] = (dot(tables[0], rows[...], NN) * LOSS_GRAD).astype(BF)
    own[...] = (dot(tables[1], rows[...], NN) * LOSS_GRAD).astype(BF)


def encgrad_body(got, at, *refs):
    chunks, (own, other, gram, rows, sem) = refs[:9], refs[9:]
    copies = load_rows(chunks, rows, sem)
    grad = jnp.where(at[...] >= 0, total(got, 0, 128) * LOSS_GRAD, 0.0)
    for d in range(NY):
        gram[16 * d : 16 * d + 16, :] = got[d, 128:144, :].astype(F32) + got[d, 144:160, :].astype(F32)
    tables, sums = [], []
    ones = jnp.ones((8, 128), F32)
    for half in (1, 0):
        parts = []
        for q in range(4):
            pieces = turned_table(at, grad, 4 * half + q)
            acc = pieces[0]
            for piece in pieces[1:]:
                acc = acc + piece
            sums.append(lax.dot_general(ones, acc, NT, precision=lax.Precision.HIGHEST, preferred_element_type=F32))
            parts.append(jnp.concatenate(pieces, axis=1).astype(BF))
        tables.append(jnp.concatenate(parts, axis=0))
    for copy in copies:
        copy.wait()
    for k, out in ((0, other), (1, own)):
        part = dot(tables[k], rows[...], NN).astype(BF)
        for q in range(4):
            out[q, 0:R, :] = part[q * R : (q + 1) * R, :]
            out[q, R : R + 8, 0:128] = sums[4 * k + q].astype(BF)
            out[q, R : R + 8, 128:1024] = jnp.zeros((8, 896), BF)


def penalty_body(count, gram_ref, decoder, out):
    gram = gram_ref[...]
    row, col = rows_iota((R, R)), lanes_iota((R, R))
    diagonal = row == col
    kept = jnp.where(diagonal, gram, 0.0)
    norm_c = jnp.sqrt(jnp.sum(kept, axis=1, keepdims=True) + EPSILON)
    norm_r = jnp.sqrt(jnp.sum(kept, axis=0, keepdims=True) + EPSILON)
    live = count[0] * BLOCK
    pair = norm_c * norm_r
    cosine = gram / pair
    alive = (row < live) & (col < live) & jnp.logical_not(diagonal)
    coupled = jnp.where(alive, cosine, 0.0)
    spread = jnp.sum(coupled * cosine, axis=1, keepdims=True)
    diag_term = jnp.where(diagonal, spread / (norm_c * norm_c), 0.0)
    weights = (4.0 * COHERENCE * (coupled / pair - diag_term)).astype(BF)
    out[...] = dot(weights, decoder[...], NN)


def add(a, b):
    return (a.astype(F32) + b.astype(F32)).astype(BF)


def gather_z(own, cut):
    f1, b1 = move(own, dz=1), move(own, dz=-1)
    f2, b2 = move(f1, dz=1), move(b1, dz=-1)
    f3, b3 = move(f2, dz=1), move(b2, dz=-1)
    f4, b4 = move(f3[:cut], dz=1), move(b3[cut:], dz=-1)
    return [own, f1, b1, f2, b2, f3, b3, f4, b4]


def scatter_x(own, other):
    theirs = move(other, dc=1)
    blocks = [add(own[i], theirs[i]) for i in range(4)]
    cut = 64
    f = move(blocks[3][:cut], dx=1)
    b = move(blocks[3][cut:], dx=-1)
    to_next = jnp.concatenate([add(blocks[2][:cut], f), blocks[2][cut:]], axis=0)
    to_prev = jnp.concatenate([blocks[1][:cut], add(blocks[1][cut:], b)], axis=0)
    return blocks[0], move(to_next, dx=1), move(to_prev, dx=-1)


def per_device(tokens, dec_bias, encoder, enc_bias, decoder, atom_ids, block_count):
    place = lax.axis_index("atoms")
    pos = jnp.stack([place // (NZ * NC), (place // NC) % NZ, place % NC]).astype(I32)
    bias_row = dec_bias.reshape(1, -1)

    sent = call(center_body, sds((R + 8, 1024), BF), tokens, bias_row, atom_ids, specs=whole(3), name="center")
    packed, gram_part = call(
        pack_body,
        (sds((2 * R + 8, 1024), BF), sds((R, R), F32)),
        encoder, decoder, enc_bias.reshape(1, -1), specs=whole(3), name="pack",
    )
    tok = gather_z(sent, 64)

    x1, x2 = move(packed, dx=1), move(packed, dx=-1)
    x3e, x3d = move(x1[:R], dx=1), move(x2[R:], dx=-1)
    enc_own = jnp.concatenate([encoder, x1[:R], x2[:R], x3e], axis=0)
    dec_own = jnp.concatenate(
        [decoder, x1[R : 2 * R], x2[R : 2 * R], x3d[:R], packed[2 * R :], x1[2 * R :], x2[2 * R :], x3d[R:]], axis=0
    )
    enc_other = move(enc_own, dc=1)
    dec_other = move(dec_own, dc=1)

    def score(chunks, split=False):
        n = 1 if split else len(chunks)
        return call(
            score_body(split, n),
            (sds((16 * n, 128), F32), sds((16 * n, 128), I32)),
            pos, enc_own, enc_other, *chunks,
            specs=[SMEM_SPEC] + whole(2 + len(chunks)), name="score",
        )

    picks, wheres = zip(score(tok[0:3]), score(tok[3:5]), score(tok[5:7]), score(tok[7:9], True))
    out = call(send_body, sds((NY, 160, 128), BF), *picks, gram_part, specs=whole(5), name="send")
    got = lax.all_to_all(out, "width", split_axis=0, concat_axis=0, tiled=True)

    act, where, at_t, act_t, gram_rows, d7 = call(
        act_body,
        (sds((R, R), F32), sds((R, R), I32), sds((R, R), I32), sds((R, R), F32), sds((32, 128), BF), sds((R, 1024), BF)),
        got, dec_own, dec_other, *wheres, specs=whole(7), name="act",
    )

    def decoded(ms, dtype=BF):
        return call(
            decode_body(ms), tuple(sds((R, 1024), dtype) for _ in ms),
            at_t, act_t, dec_own, dec_other, specs=whole(4), name="decode",
        )

    d5, d6 = decoded((5, 6))
    d3, d4 = decoded((3, 4))
    d1, d2 = decoded((1, 2))
    (d0,) = decoded((0,), F32)
    f = move(d7[:64], dz=1)
    b = move(d7[64:], dz=-1)
    f = move(jnp.concatenate([add(d6[:64], f), d6[64:]], axis=0), dz=1)
    b = move(jnp.concatenate([d5[:64], add(d5[64:], b)], axis=0), dz=-1)
    f, b = move(add(d4, f), dz=1), move(add(d3, b), dz=-1)
    f, b = move(add(d2, f), dz=1), move(add(d1, b), dz=-1)
    summed = d0 + f.astype(F32) + b.astype(F32)
    residual = (summed + bias_row - tokens.astype(F32)).astype(BF)

    res = gather_z(residual, 64)

    def back(chunks, first, split=False):
        n = 1 if split else len(chunks)
        return call(
            back_body(split, n, first), sds((16 * n, 128), F32),
            dec_own, dec_other, where, *chunks, specs=whole(3 + len(chunks)), name="back",
        )

    backs = (back(res[0:3], 0), back(res[3:5], 3), back(res[5:7], 5), back(res[7:9], 7, True))
    out2 = call(resend_body, sds((NY, 160, 128), BF), *backs, gram_rows, specs=whole(5), name="resend")
    got2 = lax.all_to_all(out2, "width", split_axis=0, concat_axis=0, tiled=True)

    scratch = [pltpu.VMEM((8 * R, 1024), BF), pltpu.SemaphoreType.DMA((9,))]
    fit_own, fit_other = call(
        fitted_body, (sds((4 * R, 1024), BF), sds((4 * R, 1024), BF)),
        where, act, *res, specs=whole(2) + [ANY_SPEC] * 9, scratch=scratch, name="fitted",
    )
    fit = scatter_x(fit_own.reshape(4, R, 1024), fit_other.reshape(4, R, 1024))

    eg_own, eg_other, gram = call(
        encgrad_body, (sds((4, R + 8, 1024), BF), sds((4, R + 8, 1024), BF), sds((R, R), F32)),
        got2, where, *tok, specs=whole(2) + [ANY_SPEC] * 9, scratch=scratch, name="encgrad",
    )
    eg = scatter_x(eg_own, eg_other)
    eg_sum = eg[0].astype(F32) + eg[1].astype(F32) + eg[2].astype(F32)
    encoder_grad = eg_sum[:R].astype(BF)
    bias_grad = eg_sum[R, 0:R]

    penalty = call(
        penalty_body, sds((R, 1024), F32), block_count, gram, decoder, specs=[SMEM_SPEC] + whole(2), name="penalty"
    )
    decoder_grad = (fit[0].astype(F32) + fit[1].astype(F32) + fit[2].astype(F32) + penalty).astype(BF)
    return (residual, encoder_grad, decoder_grad, bias_grad)


def solution(mesh):
    in_specs = (
        P("atoms", "width"),
        P("width"),
        P("atoms", "width"),
        P("atoms"),
        P("atoms", "width"),
        P("atoms", None),
        P("atoms"),
    )
    out_specs = (P("atoms", "width"), P("atoms", "width"), P("atoms", "width"), P("atoms"))
    return jax.shard_map(per_device, mesh=mesh, in_specs=in_specs, out_specs=out_specs, check_vma=False)
```

```python
import jax
import jax.numpy as jnp
from jax import lax
from jax.experimental import pallas as pl
from jax.experimental.pallas import tpu as pltpu
from jax.sharding import PartitionSpec as P

NX, NZ, NC, NY = 4, 8, 2, 8
BLOCK = 64
R = 128
COHERENCE = 128.0
LOSS_GRAD = 1.0 / 32.0
EPSILON = 1e-06
BF, F32, I32 = jnp.bfloat16, jnp.float32, jnp.int32
VMEM = 20 * 1024 * 1024
CAP = 24


def _place(x, z, c):
    return ((x % NX) * NZ + z % NZ) * NC + c % NC


def _perm(dx=0, dz=0, dc=0):
    return [
        (_place(x, z, c), _place(x + (dx if c == 0 else -dx), z + (dz if c == 0 else -dz), c + dc))
        for x in range(NX)
        for z in range(NZ)
        for c in range(NC)
    ]


def move(value, **shift):
    return lax.ppermute(value, "atoms", _perm(**shift))


def call(body, outs, *args, scratch=(), specs=None, name):
    return pl.pallas_call(
        body,
        out_shape=outs,
        in_specs=specs,
        scratch_shapes=scratch,
        compiler_params=pltpu.CompilerParams(vmem_limit_bytes=VMEM),
        name=name,
    )(*args)


def sds(shape, dtype):
    return jax.ShapeDtypeStruct(shape, dtype)


def whole(n):
    return [pl.BlockSpec(memory_space=pltpu.VMEM)] * n


SMEM_SPEC = pl.BlockSpec(memory_space=pltpu.SMEM)
ANY_SPEC = pl.BlockSpec(memory_space=pl.ANY)

NT = (((1,), (1,)), ((), ()))
NN = (((1,), (0,)), ((), ()))


def dot(a, b, dims):
    return lax.dot_general(a, b, dims, preferred_element_type=F32)


def rows_iota(shape):
    return lax.broadcasted_iota(I32, shape, 0)


def lanes_iota(shape):
    return lax.broadcasted_iota(I32, shape, 1)


def center_body(tokens, dec_bias, atom_ids, out):
    out[0:R, :] = (tokens[...].astype(F32) - dec_bias[...]).astype(BF)
    ids = atom_ids[...]
    owner = (ids >> 7).astype(F32).astype(BF)
    local = (ids & 127).astype(F32).astype(BF)
    row, col = rows_iota((8, 16)), lanes_iota((8, 16))
    even = (col == 2 * row).astype(F32).astype(BF)
    odd = (col == 2 * row + 1).astype(F32).astype(BF)
    out[R : R + 8, 0:128] = dot(even, owner, NT).astype(BF)
    out[R : R + 8, 128:256] = dot(even, local, NT).astype(BF)
    out[R : R + 8, 256:384] = dot(odd, local, NT).astype(BF)
    out[R : R + 8, 384:1024] = jnp.zeros((8, 640), BF)


def pack_body(encoder, decoder, enc_bias, after, out, gram):
    out[0:R, :] = encoder[...]
    out[R : 2 * R, :] = decoder[...]
    bias = jnp.broadcast_to(enc_bias[...], (8, 128))
    high = bias.astype(BF)
    rest = bias - high.astype(F32)
    mid = rest.astype(BF)
    low = (rest - mid.astype(F32)).astype(BF)
    out[2 * R : 2 * R + 8, 0:128] = high
    out[2 * R : 2 * R + 8, 128:256] = mid
    out[2 * R : 2 * R + 8, 256:384] = low
    out[2 * R : 2 * R + 8, 384:1024] = jnp.zeros((8, 640), BF)
    gram[...] = dot(decoder[...], decoder[...], NT)


def locate(ext, pos):
    x, z, c = pos[0], pos[1], pos[2]
    owner = ext[:, 0:128].astype(I32)
    first, second = ext[:, 128:256].astype(I32), ext[:, 256:384].astype(I32)
    dx = (((owner >> 4) - x) * (1 - 2 * (owner & 1)) + NX) & 3
    b = jnp.where(dx == 0, 0, jnp.where(dx == 3, 1, jnp.where(dx == 1, 2, 3)))
    b = b + jnp.where((owner & 1) == c, 0, 4)
    b = jnp.where(((owner >> 1) & 7) == z, b, -1)
    slot = rows_iota((8, 128))
    at_a = jnp.full((8, 128), -1, I32)
    at_b = jnp.full((8, 128), -1, I32)
    for g in range(8):
        hit = jnp.broadcast_to(b[g : g + 1, :], (8, 128)) == slot
        at_a = jnp.where(hit, jnp.broadcast_to(first[g : g + 1, :], (8, 128)), at_a)
        at_b = jnp.where(hit, jnp.broadcast_to(second[g : g + 1, :], (8, 128)), at_b)
    return at_a, at_b


def pick_into(out, tables, tok, places):
    n = len(places)
    atom = rows_iota((R, 128))
    for h, table in enumerate(tables):
        scores = dot(table[0 : 4 * R, :], tok, NT)
        for i in range(n):
            at_a, at_b = places[i]
            for q in range(4):
                b = 4 * h + q
                part = scores[q * R : (q + 1) * R, i * 128 : (i + 1) * 128]
                for s, at in ((0, at_a), (1, at_b)):
                    row = jnp.broadcast_to(at[b : b + 1, :], (R, 128))
                    got = jnp.sum(jnp.where(atom == row, part, 0.0), axis=0, keepdims=True)
                    out[16 * i + 8 * s + b : 16 * i + 8 * s + b + 1, :] = got


def score_body(pos, own, other, *refs):
    chunks, (picks, where) = refs[:-2], refs[-2:]
    places = [locate(c[R : R + 8, 0:384].astype(F32), pos) for c in chunks]
    for i, (at_a, at_b) in enumerate(places):
        where[16 * i : 16 * i + 8, :] = at_a
        where[16 * i + 8 : 16 * i + 16, :] = at_b
    toks = [c[0:R, :] for c in chunks]
    tok = toks[0] if len(toks) == 1 else jnp.concatenate(toks, axis=0)
    pick_into(picks, (own, other), tok, places)


def back_body(first):
    def body(own, other, where, *refs):
        chunks, picks = refs[:-1], refs[-1]
        toks = [c[...] for c in chunks]
        places = []
        for i in range(len(chunks)):
            at = 16 * (first + i)
            places.append((where[at : at + 8, :], where[at + 8 : at + 16, :]))
        tok = toks[0] if len(toks) == 1 else jnp.concatenate(toks, axis=0)
        pick_into(picks, (own, other), tok, places)

    return body


def halves_of(packed):
    first = jnp.concatenate([packed[16 * m : 16 * m + 8, :] for m in range(8)], axis=0)
    second = jnp.concatenate([packed[16 * m + 8 : 16 * m + 16, :] for m in range(8)], axis=0)
    return first, second


def squeeze(picks, live, rank):
    first, second = halves_of(picks)
    lane = lanes_iota((64, 128))
    left = jnp.where(live, lane - rank, 0)
    for k in range(7):
        step = 128 - (1 << k)
        left_in = pltpu.roll(left, step, 1)
        hit = ((left_in >> k) & 1) == 1
        first = jnp.where(hit, pltpu.roll(first, step, 1), first)
        second = jnp.where(hit, pltpu.roll(second, step, 1), second)
        left = jnp.where(hit, left_in, jnp.where(((left >> k) & 1) == 1, 0, left))
    lane = lanes_iota((32, 128))
    out = jnp.zeros((32, 128), F32)
    for q, part in enumerate((first[0:32], first[32:64], second[0:32], second[32:64])):
        moved = part if q == 0 else pltpu.roll(part, 32 * q, 1)
        out = jnp.where((lane >> 5) == q, moved, out)
    return out


def unsqueeze(got, rank):
    parts = [got] + [pltpu.roll(got, 128 - 32 * q, 1) for q in (1, 2, 3)]
    first = jnp.concatenate(parts[0:2], axis=0)
    second = jnp.concatenate(parts[2:4], axis=0)
    index = jnp.minimum(rank, CAP - 1)
    out = []
    for m in range(8):
        for half in (first, second):
            out.append(
                jnp.take_along_axis(
                    half[8 * m : 8 * m + 8, :], index[8 * m : 8 * m + 8, :], axis=1, mode="promise_in_bounds"
                )
            )
    return jnp.concatenate(out, axis=0)


def send_body(p0, p1, w0, w1, gram, out, where, ranks):
    picks = jnp.concatenate([p0[...], p1[...]], axis=0)
    at = jnp.concatenate([w0[...], w1[...]], axis=0)
    where[...] = at
    live = halves_of(at)[0] >= 0
    before = (rows_iota((128, 128)) < lanes_iota((128, 128))).astype(F32).astype(BF)
    rank = dot(jnp.where(live, 1.0, 0.0).astype(BF), before, NN).astype(I32)
    ranks[...] = rank
    sent = squeeze(picks, live, rank).astype(BF)
    high = gram[...].astype(BF)
    low = (gram[...] - high.astype(F32)).astype(BF)
    for d in range(NY):
        out[d, 0:32, :] = sent
        out[d, 32:48, :] = high[16 * d : 16 * d + 16, :]
        out[d, 48:64, :] = low[16 * d : 16 * d + 16, :]


def resend_body(p0, p1, where, ranks, rows, out):
    picks = jnp.concatenate([p0[...], p1[...]], axis=0)
    live = halves_of(where[...])[0] >= 0
    sent = squeeze(picks, live, ranks[...]).astype(BF)
    for d in range(NY):
        out[d, 0:32, :] = sent
        out[d, 32:64, :] = rows[...]


def total(got, lo, hi):
    acc = got[0, lo:hi, :].astype(F32)
    for d in range(1, NY):
        acc = acc + got[d, lo:hi, :].astype(F32)
    return acc


def table_rows(at_t, val_t, m, half):
    lane = lanes_iota((R, 128))
    parts = []
    for q in range(4):
        k = 16 * m + 4 * half + q
        first = jnp.where(lane == at_t[:, k : k + 1], val_t[:, k : k + 1], 0.0)
        second = jnp.where(lane == at_t[:, k + 8 : k + 9], val_t[:, k + 8 : k + 9], 0.0)
        parts.append((first + second).astype(BF))
    return jnp.concatenate(parts, axis=1)


def decode(at_t, val_t, own, other, ms):
    halves = []
    for half, table in enumerate((own, other)):
        rows = [table_rows(at_t, val_t, m, half) for m in ms]
        rows = rows[0] if len(ms) == 1 else jnp.concatenate(rows, axis=0)
        halves.append(dot(rows, table[0 : 4 * R, :], NN))
    return halves[0] + halves[1]


def act_body(got, own, other, where, ranks, act, at_t, act_t, gram_rows, out):
    pre = unsqueeze(total(got, 0, 32), ranks[...])
    bias = []
    for table in (own, other):
        for q in range(4):
            ext = table[4 * R + 8 * q : 4 * R + 8 * q + 8, 0:384].astype(F32)
            bias.append((ext[0:1, 0:128] + ext[0:1, 128:256]) + ext[0:1, 256:384])
    bias = jnp.concatenate(bias, axis=0)
    at = where[...]
    shift = [
        jnp.take_along_axis(bias, jnp.maximum(at[8 * k : 8 * k + 8, :], 0), axis=1, mode="promise_in_bounds")
        for k in range(16)
    ]
    pre = pre + jnp.concatenate(shift, axis=0)
    value = jnp.where(at >= 0, pre.astype(BF).astype(F32), 0.0)
    act[...] = value
    turned = at.astype(F32).T.astype(I32)
    value_t = value.T
    at_t[...] = turned
    act_t[...] = value_t
    rows = total(got, 32, 48) + total(got, 48, 64)
    high = rows.astype(BF)
    gram_rows[0:16, :] = high
    gram_rows[16:32, :] = (rows - high.astype(F32)).astype(BF)
    out[...] = decode(turned, value_t, own, other, (7,)).astype(BF)


def decode_body(ms):
    def body(at_t, act_t, own, other, *outs):
        got = decode(at_t[...], act_t[...], own, other, ms)
        for i, out in enumerate(outs):
            out[...] = got[i * R : (i + 1) * R, :].astype(out.dtype)

    return body


def turned_table(at, val, b):
    atom = rows_iota((R, 128))
    parts = []
    for m in range(8):
        k = 16 * m + b
        first = jnp.where(atom == at[k : k + 1, :], val[k : k + 1, :], 0.0)
        second = jnp.where(atom == at[k + 8 : k + 9, :], val[k + 8 : k + 9, :], 0.0)
        parts.append(first + second)
    return parts


def load_rows(refs, rows, sem):
    copies = [
        pltpu.make_async_copy(ref.at[pl.ds(0, R)], rows.at[pl.ds(i * R, R)], sem.at[i]) for i, ref in enumerate(refs)
    ]
    for copy in copies:
        copy.start()
    return copies


def fitted_body(half):
    def body(at, act, after, *refs):
        chunks, (out, rows, sem) = refs[:8], refs[8:]
        copies = load_rows(chunks, rows, sem)
        parts = [jnp.concatenate(turned_table(at, act, 4 * half + q), axis=1).astype(BF) for q in range(4)]
        table = jnp.concatenate(parts, axis=0)
        for copy in copies:
            copy.wait()
        out[...] = (dot(table, rows[...], NN) * LOSS_GRAD).astype(BF)

    return body


def encgrad_body(half):
    def body(got, at, ranks, *refs):
        chunks, rest = refs[:8], refs[8:]
        out, (rows, sem) = rest[0], rest[-2:]
        copies = load_rows(chunks, rows, sem)
        grad = jnp.where(at[...] >= 0, unsqueeze(total(got, 0, 32), ranks[...]) * LOSS_GRAD, 0.0)
        if half == 0:
            gram = rest[1]
            for d in range(NY):
                gram[16 * d : 16 * d + 16, :] = got[d, 32:48, :].astype(F32) + got[d, 48:64, :].astype(F32)
        parts, ones = [], jnp.ones((8, 128), F32)
        for q in range(4):
            pieces = turned_table(at, grad, 4 * half + q)
            acc = pieces[0]
            for piece in pieces[1:]:
                acc = acc + piece
            sums = lax.dot_general(ones, acc, NT, precision=lax.Precision.HIGHEST, preferred_element_type=F32)
            out[q, R : R + 8, 0:128] = sums.astype(BF)
            out[q, R : R + 8, 128:1024] = jnp.zeros((8, 896), BF)
            parts.append(jnp.concatenate(pieces, axis=1).astype(BF))
        table = jnp.concatenate(parts, axis=0)
        for copy in copies:
            copy.wait()
        part = dot(table, rows[...], NN).astype(BF)
        for q in range(4):
            out[q, 0:R, :] = part[q * R : (q + 1) * R, :]

    return body


def penalty_body(count, gram_ref, decoder, out):
    gram = gram_ref[...]
    row, col = rows_iota((R, R)), lanes_iota((R, R))
    diagonal = row == col
    kept = jnp.where(diagonal, gram, 0.0)
    norm_c = jnp.sqrt(jnp.sum(kept, axis=1, keepdims=True) + EPSILON)
    norm_r = jnp.sqrt(jnp.sum(kept, axis=0, keepdims=True) + EPSILON)
    live = count[0] * BLOCK
    pair = norm_c * norm_r
    cosine = gram / pair
    alive = (row < live) & (col < live) & jnp.logical_not(diagonal)
    coupled = jnp.where(alive, cosine, 0.0)
    spread = jnp.sum(coupled * cosine, axis=1, keepdims=True)
    diag_term = jnp.where(diagonal, spread / (norm_c * norm_c), 0.0)
    weights = (4.0 * COHERENCE * (coupled / pair - diag_term)).astype(BF)
    out[...] = dot(weights, decoder[...], NN)


def add(a, b):
    return (a.astype(F32) + b.astype(F32)).astype(BF)


def gather_z(own):
    f1, b1 = move(own, dz=1), move(own, dz=-1)
    f2, b2 = move(f1, dz=1), move(b1, dz=-1)
    f3, b3 = move(f2, dz=1), move(b2, dz=-1)
    return [own, f1, b1, f2, b2, f3, b3, move(f3, dz=1)]


def scatter_x(own, theirs):
    blocks = [add(own[i], theirs[i]) for i in range(4)]
    to_next = add(blocks[2], move(blocks[3], dx=1))
    return blocks[0], move(blocks[1], dx=-1), move(to_next, dx=1)


def per_device(tokens, dec_bias, encoder, enc_bias, decoder, atom_ids, block_count):
    place = lax.axis_index("atoms")
    pos = jnp.stack([place >> 4, (place >> 1) & 7, place & 1]).astype(I32)
    bias_row = dec_bias.reshape(1, -1)

    sent = call(center_body, sds((R + 8, 1024), BF), tokens, bias_row, atom_ids, specs=whole(3), name="center")
    packed, gram_part = call(
        pack_body,
        (sds((2 * R + 8, 1024), BF), sds((R, R), F32)),
        encoder, decoder, enc_bias.reshape(1, -1), sent, specs=whole(3) + [ANY_SPEC], name="pack",
    )
    tok = gather_z(sent)

    x1, x2 = move(packed, dx=1), move(packed, dx=-1)
    x3 = move(x1, dx=1)
    enc_own = jnp.concatenate([encoder, x1[:R], x2[:R], x3[:R]], axis=0)
    dec_own = jnp.concatenate(
        [decoder, x1[R : 2 * R], x2[R : 2 * R], x3[R : 2 * R], packed[2 * R :], x1[2 * R :], x2[2 * R :], x3[2 * R :]],
        axis=0,
    )
    enc_other = move(enc_own, dc=1)
    dec_other = move(dec_own, dc=1)

    def score(chunks):
        n = len(chunks)
        return call(
            score_body,
            (sds((16 * n, 128), F32), sds((16 * n, 128), I32)),
            pos, enc_own, enc_other, *chunks,
            specs=[SMEM_SPEC] + whole(2 + n), name="score",
        )

    picks, wheres = zip(score(tok[0:7]), score(tok[7:8]))
    out, where, ranks = call(
        send_body, (sds((NY, 64, 128), BF), sds((R, R), I32), sds((64, R), I32)),
        *picks, *wheres, gram_part, specs=whole(5), name="send",
    )
    got = lax.all_to_all(out, "width", split_axis=0, concat_axis=0, tiled=True)

    act, at_t, act_t, gram_rows, d7 = call(
        act_body,
        (sds((R, R), F32), sds((R, R), I32), sds((R, R), F32), sds((32, 128), BF), sds((R, 1024), BF)),
        got, dec_own, dec_other, where, ranks, specs=whole(5), name="act",
    )

    def decoded(ms, dtype=BF):
        return call(
            decode_body(ms), tuple(sds((R, 1024), dtype) for _ in ms),
            at_t, act_t, dec_own, dec_other, specs=whole(4), name="decode",
        )

    d5, d6 = decoded((5, 6))
    d3, d4 = decoded((3, 4))
    d1, d2 = decoded((1, 2))
    (d0,) = decoded((0,), F32)
    f = move(d7, dz=1)
    b = move(d5, dz=-1)
    f = move(add(d6, f), dz=1)
    b = move(add(d3, b), dz=-1)
    f = move(add(d4, f), dz=1)
    b = move(add(d1, b), dz=-1)
    f = move(add(d2, f), dz=1)
    summed = d0 + f.astype(F32) + b.astype(F32)
    residual = (summed + bias_row - tokens.astype(F32)).astype(BF)

    res = gather_z(residual)

    def back(chunks, first):
        n = len(chunks)
        return call(
            back_body(first), sds((16 * n, 128), F32),
            dec_own, dec_other, where, *chunks, specs=whole(3 + n), name="back",
        )

    backs = (back(res[0:7], 0), back(res[7:8], 7))
    out2 = call(
        resend_body, sds((NY, 64, 128), BF), *backs, where, ranks, gram_rows, specs=whole(5), name="resend"
    )
    got2 = lax.all_to_all(out2, "width", split_axis=0, concat_axis=0, tiled=True)

    scratch = [pltpu.VMEM((8 * R, 1024), BF), pltpu.SemaphoreType.DMA((8,))]

    def fitted(half, after):
        return call(
            fitted_body(half), sds((4 * R, 1024), BF), where, act, after, *res,
            specs=whole(2) + [ANY_SPEC] * 9, scratch=scratch, name="fitted",
        )

    fit_other = fitted(1, out2)
    fit_theirs = move(fit_other, dc=1)
    fit_own = fitted(0, fit_other)
    fit = scatter_x(fit_own.reshape(4, R, 1024), fit_theirs.reshape(4, R, 1024))

    def encgrad(half):
        outs = [sds((4, R + 8, 1024), BF)] + ([sds((R, R), F32)] if half == 0 else [])
        return call(
            encgrad_body(half), tuple(outs), got2, where, ranks, *tok,
            specs=whole(3) + [ANY_SPEC] * 8, scratch=scratch, name="encgrad",
        )

    (eg_other,) = encgrad(1)
    eg_theirs = move(eg_other, dc=1)
    eg_own, gram = encgrad(0)
    eg = scatter_x(eg_own, eg_theirs)
    eg_sum = eg[0].astype(F32) + eg[1].astype(F32) + eg[2].astype(F32)
    encoder_grad = eg_sum[:R].astype(BF)
    bias_grad = eg_sum[R, 0:R]

    penalty = call(
        penalty_body, sds((R, 1024), F32), block_count, gram, decoder, specs=[SMEM_SPEC] + whole(2), name="penalty"
    )
    decoder_grad = (fit[0].astype(F32) + fit[1].astype(F32) + fit[2].astype(F32) + penalty).astype(BF)
    return (residual, encoder_grad, decoder_grad, bias_grad)


def solution(mesh):
    in_specs = (
        P("atoms", "width"),
        P("width"),
        P("atoms", "width"),
        P("atoms"),
        P("atoms", "width"),
        P("atoms", None),
        P("atoms"),
    )
    out_specs = (P("atoms", "width"), P("atoms", "width"), P("atoms", "width"), P("atoms"))
    return jax.shard_map(per_device, mesh=mesh, in_specs=in_specs, out_specs=out_specs, check_vma=False)
```

```python
import jax
import jax.numpy as jnp
from jax import lax
from jax.experimental import pallas as pl
from jax.experimental.pallas import tpu as pltpu
from jax.sharding import PartitionSpec as P

NX, NZ, NC, NY = 4, 8, 2, 8
BLOCK = 64
R = 128
COHERENCE = 128.0
LOSS_GRAD = 1.0 / 32.0
EPSILON = 1e-06
BF, F32, I32 = jnp.bfloat16, jnp.float32, jnp.int32
VMEM = 20 * 1024 * 1024
CAP = 24


def _place(x, z, c):
    return ((x % NX) * NZ + z % NZ) * NC + c % NC


def _side(place, core):
    return 1 if (place + core) % 2 == 0 else -1


def _swap(axis, partner):
    pairs = []
    for x in range(NX):
        for z in range(NZ):
            for c in range(NC):
                if axis == "x":
                    to = _place(x + partner * _side(x, c), z, c)
                elif axis == "z":
                    to = _place(x, z + partner * _side(z, c), c)
                else:
                    to = _place(x, z, c + 1)
                pairs.append((_place(x, z, c), to))
    return pairs


def swap(value, axis, partner=1):
    return lax.ppermute(value, "atoms", _swap(axis, partner))


def call(body, outs, *args, scratch=(), specs=None, name):
    return pl.pallas_call(
        body,
        out_shape=outs,
        in_specs=specs,
        scratch_shapes=scratch,
        compiler_params=pltpu.CompilerParams(vmem_limit_bytes=VMEM),
        name=name,
    )(*args)


def sds(shape, dtype):
    return jax.ShapeDtypeStruct(shape, dtype)


def whole(n):
    return [pl.BlockSpec(memory_space=pltpu.VMEM)] * n


SMEM_SPEC = pl.BlockSpec(memory_space=pltpu.SMEM)
ANY_SPEC = pl.BlockSpec(memory_space=pl.ANY)

NT = (((1,), (1,)), ((), ()))
NN = (((1,), (0,)), ((), ()))


def dot(a, b, dims):
    return lax.dot_general(a, b, dims, preferred_element_type=F32)


def rows_iota(shape):
    return lax.broadcasted_iota(I32, shape, 0)


def lanes_iota(shape):
    return lax.broadcasted_iota(I32, shape, 1)


def center_body(tokens, dec_bias, atom_ids, out):
    out[0:R, :] = (tokens[...].astype(F32) - dec_bias[...]).astype(BF)
    ids = atom_ids[...]
    owner = (ids >> 7).astype(F32).astype(BF)
    local = (ids & 127).astype(F32).astype(BF)
    row, col = rows_iota((8, 16)), lanes_iota((8, 16))
    even = (col == 2 * row).astype(F32).astype(BF)
    odd = (col == 2 * row + 1).astype(F32).astype(BF)
    out[R : R + 8, 0:128] = dot(even, owner, NT).astype(BF)
    out[R : R + 8, 128:256] = dot(even, local, NT).astype(BF)
    out[R : R + 8, 256:384] = dot(odd, local, NT).astype(BF)
    out[R : R + 8, 384:1024] = jnp.zeros((8, 640), BF)


def pack_body(encoder, decoder, enc_bias, after, out, gram):
    out[0:R, :] = encoder[...]
    out[R : 2 * R, :] = decoder[...]
    bias = jnp.broadcast_to(enc_bias[...], (8, 128))
    high = bias.astype(BF)
    rest = bias - high.astype(F32)
    mid = rest.astype(BF)
    low = (rest - mid.astype(F32)).astype(BF)
    out[2 * R : 2 * R + 8, 0:128] = high
    out[2 * R : 2 * R + 8, 128:256] = mid
    out[2 * R : 2 * R + 8, 256:384] = low
    out[2 * R : 2 * R + 8, 384:1024] = jnp.zeros((8, 640), BF)
    gram[...] = dot(decoder[...], decoder[...], NT)


def locate(ext, pos):
    x, z, c = pos[0], pos[1], pos[2]
    owner = ext[:, 0:128].astype(I32)
    first, second = ext[:, 128:256].astype(I32), ext[:, 256:384].astype(I32)
    side = (1 - 2 * (owner & 1)) * (1 - 2 * (x & 1))
    dx = (((owner >> 4) - x) * side + NX) & 3
    b = jnp.where(dx == 3, 2, jnp.where(dx == 2, 3, dx))
    b = b + jnp.where((owner & 1) == c, 0, 4)
    b = jnp.where(((owner >> 1) & 7) == z, b, -1)
    slot = rows_iota((8, 128))
    at_a = jnp.full((8, 128), -1, I32)
    at_b = jnp.full((8, 128), -1, I32)
    for g in range(8):
        hit = jnp.broadcast_to(b[g : g + 1, :], (8, 128)) == slot
        at_a = jnp.where(hit, jnp.broadcast_to(first[g : g + 1, :], (8, 128)), at_a)
        at_b = jnp.where(hit, jnp.broadcast_to(second[g : g + 1, :], (8, 128)), at_b)
    return at_a, at_b


def pick_into(out, tables, tok, places):
    n = len(places)
    atom = rows_iota((R, 128))
    for h, table in enumerate(tables):
        scores = dot(table[0 : 4 * R, :], tok, NT)
        for i in range(n):
            at_a, at_b = places[i]
            for q in range(4):
                b = 4 * h + q
                part = scores[q * R : (q + 1) * R, i * 128 : (i + 1) * 128]
                for s, at in ((0, at_a), (1, at_b)):
                    row = jnp.broadcast_to(at[b : b + 1, :], (R, 128))
                    got = jnp.sum(jnp.where(atom == row, part, 0.0), axis=0, keepdims=True)
                    out[16 * i + 8 * s + b : 16 * i + 8 * s + b + 1, :] = got


def rows_of(pairs):
    parts = [p[0 : 2 * R, :] for p in pairs]
    return parts[0] if len(parts) == 1 else jnp.concatenate(parts, axis=0)


def score_body(pos, own, other, *refs):
    pairs, (picks, where) = refs[:-2], refs[-2:]
    places = []
    for p in pairs:
        for i in range(2):
            ext = p[2 * R : 2 * R + 16, 0:384].astype(F32)
            places.append(locate(ext[8 * i : 8 * i + 8, :], pos))
    for i, (at_a, at_b) in enumerate(places):
        where[16 * i : 16 * i + 8, :] = at_a
        where[16 * i + 8 : 16 * i + 16, :] = at_b
    pick_into(picks, (own, other), rows_of(pairs), places)


def back_body(first):
    def body(own, other, where, *refs):
        pairs, picks = refs[:-1], refs[-1]
        places = []
        for i in range(2 * len(pairs)):
            at = 16 * (first + i)
            places.append((where[at : at + 8, :], where[at + 8 : at + 16, :]))
        pick_into(picks, (own, other), rows_of(pairs), places)

    return body


def join_body(cuts):
    def body(first, second, *refs):
        out, at, to = refs[-1], 0, 0
        for n in cuts:
            out[to : to + n, :] = first[at : at + n, :]
            out[to + n : to + 2 * n, :] = second[at : at + n, :]
            at, to = at + n, to + 2 * n

    return body


def tables_body(near, far, after, enc, dec):
    for i, ref in enumerate((near, far)):
        enc[2 * R * i : 2 * R * (i + 1), :] = ref[0 : 2 * R, :]
        dec[2 * R * i : 2 * R * (i + 1), :] = ref[2 * R : 4 * R, :]
        dec[4 * R + 16 * i : 4 * R + 16 * i + 16, :] = ref[4 * R : 4 * R + 16, :]


def halves_of(packed):
    first = jnp.concatenate([packed[16 * m : 16 * m + 8, :] for m in range(8)], axis=0)
    second = jnp.concatenate([packed[16 * m + 8 : 16 * m + 16, :] for m in range(8)], axis=0)
    return first, second


def squeeze(picks, live, rank):
    first, second = halves_of(picks)
    lane = lanes_iota((64, 128))
    left = jnp.where(live, lane - rank, 0)
    for k in range(7):
        step = 128 - (1 << k)
        left_in = pltpu.roll(left, step, 1)
        hit = ((left_in >> k) & 1) == 1
        first = jnp.where(hit, pltpu.roll(first, step, 1), first)
        second = jnp.where(hit, pltpu.roll(second, step, 1), second)
        left = jnp.where(hit, left_in, jnp.where(((left >> k) & 1) == 1, 0, left))
    lane = lanes_iota((32, 128))
    out = jnp.zeros((32, 128), F32)
    for q, part in enumerate((first[0:32], first[32:64], second[0:32], second[32:64])):
        moved = part if q == 0 else pltpu.roll(part, 32 * q, 1)
        out = jnp.where((lane >> 5) == q, moved, out)
    return out


def unsqueeze(got, rank):
    parts = [got] + [pltpu.roll(got, 128 - 32 * q, 1) for q in (1, 2, 3)]
    first = jnp.concatenate(parts[0:2], axis=0)
    second = jnp.concatenate(parts[2:4], axis=0)
    index = jnp.minimum(rank, CAP - 1)
    out = []
    for m in range(8):
        for half in (first, second):
            out.append(
                jnp.take_along_axis(
                    half[8 * m : 8 * m + 8, :], index[8 * m : 8 * m + 8, :], axis=1, mode="promise_in_bounds"
                )
            )
    return jnp.concatenate(out, axis=0)


def send_body(p0, p1, w0, w1, gram, out, where, ranks):
    picks = jnp.concatenate([p0[...], p1[...]], axis=0)
    at = jnp.concatenate([w0[...], w1[...]], axis=0)
    where[...] = at
    live = halves_of(at)[0] >= 0
    before = (rows_iota((128, 128)) < lanes_iota((128, 128))).astype(F32).astype(BF)
    rank = dot(jnp.where(live, 1.0, 0.0).astype(BF), before, NN).astype(I32)
    ranks[...] = rank
    sent = squeeze(picks, live, rank).astype(BF)
    high = gram[...].astype(BF)
    low = (gram[...] - high.astype(F32)).astype(BF)
    for d in range(NY):
        out[d, 0:32, :] = sent
        out[d, 32:48, :] = high[16 * d : 16 * d + 16, :]
        out[d, 48:64, :] = low[16 * d : 16 * d + 16, :]


def resend_body(p0, p1, where, ranks, rows, out):
    picks = jnp.concatenate([p0[...], p1[...]], axis=0)
    live = halves_of(where[...])[0] >= 0
    sent = squeeze(picks, live, ranks[...]).astype(BF)
    for d in range(NY):
        out[d, 0:32, :] = sent
        out[d, 32:64, :] = rows[...]


def total(got, lo, hi):
    acc = got[0, lo:hi, :].astype(F32)
    for d in range(1, NY):
        acc = acc + got[d, lo:hi, :].astype(F32)
    return acc


def table_rows(at_t, val_t, m, half):
    lane = lanes_iota((R, 128))
    parts = []
    for q in range(4):
        k = 16 * m + 4 * half + q
        first = jnp.where(lane == at_t[:, k : k + 1], val_t[:, k : k + 1], 0.0)
        second = jnp.where(lane == at_t[:, k + 8 : k + 9], val_t[:, k + 8 : k + 9], 0.0)
        parts.append((first + second).astype(BF))
    return jnp.concatenate(parts, axis=1)


def decode(at_t, val_t, own, other, ms):
    halves = []
    for half, table in enumerate((own, other)):
        rows = [table_rows(at_t, val_t, m, half) for m in ms]
        rows = rows[0] if len(ms) == 1 else jnp.concatenate(rows, axis=0)
        halves.append(dot(rows, table[0 : 4 * R, :], NN))
    return halves[0] + halves[1]


def act_body(got, own, other, where, ranks, act, at_t, act_t, gram_rows, out):
    pre = unsqueeze(total(got, 0, 32), ranks[...])
    bias = []
    for table in (own, other):
        for q in range(4):
            ext = table[4 * R + 8 * q : 4 * R + 8 * q + 8, 0:384].astype(F32)
            bias.append((ext[0:1, 0:128] + ext[0:1, 128:256]) + ext[0:1, 256:384])
    bias = jnp.concatenate(bias, axis=0)
    at = where[...]
    shift = [
        jnp.take_along_axis(bias, jnp.maximum(at[8 * k : 8 * k + 8, :], 0), axis=1, mode="promise_in_bounds")
        for k in range(16)
    ]
    pre = pre + jnp.concatenate(shift, axis=0)
    value = jnp.where(at >= 0, pre.astype(BF).astype(F32), 0.0)
    act[...] = value
    turned = at.astype(F32).T.astype(I32)
    value_t = value.T
    at_t[...] = turned
    act_t[...] = value_t
    rows = total(got, 32, 48) + total(got, 48, 64)
    high = rows.astype(BF)
    gram_rows[0:16, :] = high
    gram_rows[16:32, :] = (rows - high.astype(F32)).astype(BF)
    out[...] = decode(turned, value_t, own, other, (6, 7)).astype(BF)


def decode_body(ms):
    def body(at_t, act_t, own, other, out):
        out[...] = decode(at_t[...], act_t[...], own, other, ms).astype(out.dtype)

    return body


def turned_table(at, val, b):
    atom = rows_iota((R, 128))
    parts = []
    for m in range(8):
        k = 16 * m + b
        first = jnp.where(atom == at[k : k + 1, :], val[k : k + 1, :], 0.0)
        second = jnp.where(atom == at[k + 8 : k + 9, :], val[k + 8 : k + 9, :], 0.0)
        parts.append(first + second)
    return parts


def fitted_body(half):
    def body(at, act, after, *refs):
        pairs, out = refs[:4], refs[4]
        parts = [jnp.concatenate(turned_table(at, act, 4 * half + q), axis=1).astype(BF) for q in range(4)]
        table = jnp.concatenate(parts, axis=0)
        out[...] = (dot(table, rows_of(pairs), NN) * LOSS_GRAD).astype(BF)

    return body


def encgrad_body(half):
    def body(got, at, ranks, *refs):
        pairs, rest = refs[:4], refs[4:]
        out = rest[0]
        grad = jnp.where(at[...] >= 0, unsqueeze(total(got, 0, 32), ranks[...]) * LOSS_GRAD, 0.0)
        if half == 0:
            gram = rest[1]
            for d in range(NY):
                gram[16 * d : 16 * d + 16, :] = got[d, 32:48, :].astype(F32) + got[d, 48:64, :].astype(F32)
        parts, ones = [], jnp.ones((8, 128), F32)
        for q in range(4):
            pieces = turned_table(at, grad, 4 * half + q)
            acc = pieces[0]
            for piece in pieces[1:]:
                acc = acc + piece
            sums = lax.dot_general(ones, acc, NT, precision=lax.Precision.HIGHEST, preferred_element_type=F32)
            low = 4 * R + 8 * q
            out[low : low + 8, 0:128] = sums.astype(BF)
            out[low : low + 8, 128:1024] = jnp.zeros((8, 896), BF)
            parts.append(jnp.concatenate(pieces, axis=1).astype(BF))
        table = jnp.concatenate(parts, axis=0)
        out[0 : 4 * R, :] = dot(table, rows_of(pairs), NN).astype(BF)

    return body


def penalty_body(count, gram_ref, decoder, out):
    gram = gram_ref[...]
    row, col = rows_iota((R, R)), lanes_iota((R, R))
    diagonal = row == col
    kept = jnp.where(diagonal, gram, 0.0)
    norm_c = jnp.sqrt(jnp.sum(kept, axis=1, keepdims=True) + EPSILON)
    norm_r = jnp.sqrt(jnp.sum(kept, axis=0, keepdims=True) + EPSILON)
    live = count[0] * BLOCK
    pair = norm_c * norm_r
    cosine = gram / pair
    alive = (row < live) & (col < live) & jnp.logical_not(diagonal)
    coupled = jnp.where(alive, cosine, 0.0)
    spread = jnp.sum(coupled * cosine, axis=1, keepdims=True)
    diag_term = jnp.where(diagonal, spread / (norm_c * norm_c), 0.0)
    weights = (4.0 * COHERENCE * (coupled / pair - diag_term)).astype(BF)
    out[...] = dot(weights, decoder[...], NN)


def add(a, b):
    return (a.astype(F32) + b.astype(F32)).astype(BF)


def join(first, second, cuts, *after, name):
    n = first.shape[0]
    return call(
        join_body(cuts), sds((2 * n, 1024), BF), first, second, *after,
        specs=whole(2) + [ANY_SPEC] * len(after), name=name,
    )


def gather_z(own, cuts, name):
    near = swap(own, "z", 1)
    pairs = [join(own, near, cuts, name=name)]
    for partner in (-1, 1, -1):
        pairs.append(swap(pairs[-1], "z", partner))
    return pairs


def scatter_x(own, theirs, ext):
    a, b = 2 * R, 4 * R
    if ext:
        both = [add(own[i:j], theirs[i:j]) for i, j in ((0, a), (a, b), (b, b + 2 * ext), (b + 2 * ext, b + 4 * ext))]
        far = swap(jnp.concatenate([both[1], both[3]], axis=0), "x", -1)
        keep = jnp.concatenate([both[0][:R], both[2][:ext]], axis=0)
        give = jnp.concatenate([both[0][R:], both[2][ext:]], axis=0)
        far_keep = jnp.concatenate([far[:R], far[a : a + ext]], axis=0)
        far_give = jnp.concatenate([far[R:a], far[a + ext :]], axis=0)
    else:
        keep, give = add(own[:R], theirs[:R]), add(own[R:a], theirs[R:a])
        far = swap(add(own[a:], theirs[a:]), "x", -1)
        far_keep, far_give = far[:R], far[R:]
    return keep, far_keep, swap(add(give, far_give), "x", 1)


def per_device(tokens, dec_bias, encoder, enc_bias, decoder, atom_ids, block_count):
    place = lax.axis_index("atoms")
    pos = jnp.stack([place >> 4, (place >> 1) & 7, place & 1]).astype(I32)
    bias_row = dec_bias.reshape(1, -1)

    sent = call(center_body, sds((R + 8, 1024), BF), tokens, bias_row, atom_ids, specs=whole(3), name="center")
    packed, gram_part = call(
        pack_body,
        (sds((2 * R + 8, 1024), BF), sds((R, R), F32)),
        encoder, decoder, enc_bias.reshape(1, -1), sent, specs=whole(3) + [ANY_SPEC], name="pack",
    )
    tok = gather_z(sent, (R, 8), "join")
    x_near = swap(packed, "x", 1)
    x_pair = join(packed, x_near, (R, R, 8), tok[0], name="xjoin")
    x_far = swap(x_pair, "x", -1)
    enc_own, dec_own = call(
        tables_body, (sds((4 * R, 1024), BF), sds((4 * R + 32, 1024), BF)), x_pair, x_far, tok[2],
        specs=whole(2) + [ANY_SPEC], name="tables",
    )
    enc_other = swap(enc_own, "core")
    dec_other = swap(dec_own, "core")

    def score(pairs):
        n = 2 * len(pairs)
        return call(
            score_body,
            (sds((16 * n, 128), F32), sds((16 * n, 128), I32)),
            pos, enc_own, enc_other, *pairs,
            specs=[SMEM_SPEC] + whole(2 + len(pairs)), name="score",
        )

    picks, wheres = zip(score(tok[0:3]), score(tok[3:4]))
    out, where, ranks = call(
        send_body, (sds((NY, 64, 128), BF), sds((R, R), I32), sds((64, R), I32)),
        *picks, *wheres, gram_part, specs=whole(5), name="send",
    )
    got = lax.all_to_all(out, "width", split_axis=0, concat_axis=0, tiled=True)

    act, at_t, act_t, gram_rows, d67 = call(
        act_body,
        (sds((R, R), F32), sds((R, R), I32), sds((R, R), F32), sds((32, 128), BF), sds((2 * R, 1024), BF)),
        got, dec_own, dec_other, where, ranks, specs=whole(5), name="act",
    )

    def decoded(ms, dtype=BF):
        return call(
            decode_body(ms), sds((2 * R, 1024), dtype), at_t, act_t, dec_own, dec_other, specs=whole(4), name="decode"
        )

    d45, d23, d01 = decoded((4, 5)), decoded((2, 3)), decoded((0, 1), F32)
    part = swap(d67, "z", -1)
    part = swap(add(d45, part), "z", 1)
    far = swap(add(d23, part), "z", -1)
    near = swap(add(d01[R:], far[R:]), "z", 1)
    summed = d01[:R] + far[:R].astype(F32) + near.astype(F32)
    residual = (summed + bias_row - tokens.astype(F32)).astype(BF)

    res = gather_z(residual, (R,), "rjoin")

    def back(pairs, first):
        n = 2 * len(pairs)
        return call(
            back_body(first), sds((16 * n, 128), F32),
            dec_own, dec_other, where, *pairs, specs=whole(3 + len(pairs)), name="back",
        )

    backs = (back(res[0:3], 0), back(res[3:4], 6))
    out2 = call(
        resend_body, sds((NY, 64, 128), BF), *backs, where, ranks, gram_rows, specs=whole(5), name="resend"
    )
    got2 = lax.all_to_all(out2, "width", split_axis=0, concat_axis=0, tiled=True)

    def fitted(half, after):
        return call(
            fitted_body(half), sds((4 * R, 1024), BF), where, act, after, *res,
            specs=whole(2) + [ANY_SPEC] + whole(4), name="fitted",
        )

    fit_other = fitted(1, out2)
    fit_theirs = swap(fit_other, "core")
    fit_own = fitted(0, fit_other)
    fit = scatter_x(fit_own, fit_theirs, 0)

    def encgrad(half):
        outs = [sds((4 * R + 32, 1024), BF)] + ([sds((R, R), F32)] if half == 0 else [])
        return call(
            encgrad_body(half), tuple(outs), got2, where, ranks, *tok, specs=whole(7), name="encgrad"
        )

    (eg_other,) = encgrad(1)
    eg_theirs = swap(eg_other, "core")
    eg_own, gram = encgrad(0)
    eg = scatter_x(eg_own, eg_theirs, 8)
    eg_sum = eg[0].astype(F32) + eg[1].astype(F32) + eg[2].astype(F32)
    encoder_grad = eg_sum[:R].astype(BF)
    bias_grad = eg_sum[R, 0:R]

    penalty = call(
        penalty_body, sds((R, 1024), F32), block_count, gram, decoder, specs=[SMEM_SPEC] + whole(2), name="penalty"
    )
    decoder_grad = (fit[0].astype(F32) + fit[1].astype(F32) + fit[2].astype(F32) + penalty).astype(BF)
    return (residual, encoder_grad, decoder_grad, bias_grad)


def solution(mesh):
    in_specs = (
        P("atoms", "width"),
        P("width"),
        P("atoms", "width"),
        P("atoms"),
        P("atoms", "width"),
        P("atoms", None),
        P("atoms"),
    )
    out_specs = (P("atoms", "width"), P("atoms", "width"), P("atoms", "width"), P("atoms"))
    return jax.shard_map(per_device, mesh=mesh, in_specs=in_specs, out_specs=out_specs, check_vma=False)
```

```python
import jax
import jax.numpy as jnp
from jax import lax
from jax.experimental import pallas as pl
from jax.experimental.pallas import tpu as pltpu
from jax.sharding import PartitionSpec as P


NX, NZ, NC, NY = 4, 8, 2, 8
BLOCK = 64
R = 128
COHERENCE = 128.0
LOSS_GRAD = 1.0 / 32.0
EPSILON = 1e-06
BF, F32, I32 = jnp.bfloat16, jnp.float32, jnp.int32
VMEM = 20 * 1024 * 1024
CAP = 24


def _place(x, z, c):
    return ((x % NX) * NZ + z % NZ) * NC + c % NC


def _perm(dx=0, dz=0, dc=0):
    return [
        (_place(x, z, c), _place(x + (dx if c == 0 else -dx), z + (dz if c == 0 else -dz), c + dc))
        for x in range(NX)
        for z in range(NZ)
        for c in range(NC)
    ]


def move(value, **shift):
    return lax.ppermute(value, "atoms", _perm(**shift))


def call(body, outs, *args, scratch=(), specs=None):
    return pl.pallas_call(
        body,
        out_shape=outs,
        in_specs=specs,
        scratch_shapes=scratch,
        compiler_params=pltpu.CompilerParams(vmem_limit_bytes=VMEM),
    )(*args)


def sds(shape, dtype):
    return jax.ShapeDtypeStruct(shape, dtype)


def whole(n):
    return [pl.BlockSpec(memory_space=pltpu.VMEM)] * n


SMEM_SPEC = pl.BlockSpec(memory_space=pltpu.SMEM)
ANY_SPEC = pl.BlockSpec(memory_space=pl.ANY)

NT = (((1,), (1,)), ((), ()))
NN = (((1,), (0,)), ((), ()))


def dot(a, b, dims):
    return lax.dot_general(a, b, dims, preferred_element_type=F32)


def rows_iota(shape):
    return lax.broadcasted_iota(I32, shape, 0)


def lanes_iota(shape):
    return lax.broadcasted_iota(I32, shape, 1)


def center_body(tokens, dec_bias, atom_ids, out):
    out[0:R, :] = (tokens[...].astype(F32) - dec_bias[...]).astype(BF)
    ids = atom_ids[...]
    owner = (ids >> 7).astype(F32).astype(BF)
    local = (ids & 127).astype(F32).astype(BF)
    row, col = rows_iota((8, 16)), lanes_iota((8, 16))
    even = (col == 2 * row).astype(F32).astype(BF)
    odd = (col == 2 * row + 1).astype(F32).astype(BF)
    out[R : R + 8, 0:128] = dot(even, owner, NT).astype(BF)
    out[R : R + 8, 128:256] = dot(even, local, NT).astype(BF)
    out[R : R + 8, 256:384] = dot(odd, local, NT).astype(BF)
    out[R : R + 8, 384:1024] = jnp.zeros((8, 640), BF)


def pack_body(encoder, decoder, enc_bias, after, out, gram):
    out[0:R, :] = encoder[...]
    out[R : 2 * R, :] = decoder[...]
    bias = jnp.broadcast_to(enc_bias[...], (8, 128))
    high = bias.astype(BF)
    rest = bias - high.astype(F32)
    mid = rest.astype(BF)
    low = (rest - mid.astype(F32)).astype(BF)
    out[2 * R : 2 * R + 8, 0:128] = high
    out[2 * R : 2 * R + 8, 128:256] = mid
    out[2 * R : 2 * R + 8, 256:384] = low
    out[2 * R : 2 * R + 8, 384:1024] = jnp.zeros((8, 640), BF)
    gram[...] = dot(decoder[...], decoder[...], NT)


def locate(ext, pos):
    x, z, c = pos[0], pos[1], pos[2]
    owner = ext[:, 0:128].astype(I32)
    first, second = ext[:, 128:256].astype(I32), ext[:, 256:384].astype(I32)
    dx = (((owner >> 4) - x) * (1 - 2 * (owner & 1)) + NX) & 3
    b = jnp.where(dx == 0, 0, jnp.where(dx == 3, 1, jnp.where(dx == 1, 2, 3)))
    b = b + jnp.where((owner & 1) == c, 0, 4)
    b = jnp.where(((owner >> 1) & 7) == z, b, -1)
    slot = rows_iota((8, 128))
    at_a = jnp.full((8, 128), -1, I32)
    at_b = jnp.full((8, 128), -1, I32)
    for g in range(8):
        hit = jnp.broadcast_to(b[g : g + 1, :], (8, 128)) == slot
        at_a = jnp.where(hit, jnp.broadcast_to(first[g : g + 1, :], (8, 128)), at_a)
        at_b = jnp.where(hit, jnp.broadcast_to(second[g : g + 1, :], (8, 128)), at_b)
    return at_a, at_b


def pick_into(out, tables, tok, places):
    n = len(places)
    atom = rows_iota((R, 128))
    for h, table in enumerate(tables):
        scores = dot(table[0 : 4 * R, :], tok, NT)
        for i in range(n):
            at_a, at_b = places[i]
            for q in range(4):
                b = 4 * h + q
                part = scores[q * R : (q + 1) * R, i * 128 : (i + 1) * 128]
                for s, at in ((0, at_a), (1, at_b)):
                    row = jnp.broadcast_to(at[b : b + 1, :], (R, 128))
                    got = jnp.sum(jnp.where(atom == row, part, 0.0), axis=0, keepdims=True)
                    out[16 * i + 8 * s + b : 16 * i + 8 * s + b + 1, :] = got


def score_body(n):
    def body(pos, own, other, *refs):
        chunks, (picks, where, *rows) = refs[:n], refs[n:]
        places = [locate(c[R : R + 8, 0:384].astype(F32), pos) for c in chunks]
        for i, (at_a, at_b) in enumerate(places):
            where[16 * i : 16 * i + 8, :] = at_a
            where[16 * i + 8 : 16 * i + 16, :] = at_b
        toks = [c[0:R, :] for c in chunks]
        tok = toks[0] if n == 1 else jnp.concatenate(toks, axis=0)
        for out in rows:
            out[...] = tok
        pick_into(picks, (own, other), tok, places)

    return body


def back_body(first, n):
    def body(own, other, where, *refs):
        chunks, (picks, *rows) = refs[:n], refs[n:]
        toks = [c[...] for c in chunks]
        places = []
        for i in range(n):
            at = 16 * (first + i)
            places.append((where[at : at + 8, :], where[at + 8 : at + 16, :]))
        tok = toks[0] if n == 1 else jnp.concatenate(toks, axis=0)
        for out in rows:
            out[...] = tok
        pick_into(picks, (own, other), tok, places)

    return body


def halves_of(packed):
    first = jnp.concatenate([packed[16 * m : 16 * m + 8, :] for m in range(8)], axis=0)
    second = jnp.concatenate([packed[16 * m + 8 : 16 * m + 16, :] for m in range(8)], axis=0)
    return first, second


def squeeze(picks, live, rank):
    first, second = halves_of(picks)
    lane = lanes_iota((64, 128))
    left = jnp.where(live, lane - rank, 0)
    for k in range(7):
        step = 128 - (1 << k)
        left_in = pltpu.roll(left, step, 1)
        hit = ((left_in >> k) & 1) == 1
        first = jnp.where(hit, pltpu.roll(first, step, 1), first)
        second = jnp.where(hit, pltpu.roll(second, step, 1), second)
        left = jnp.where(hit, left_in, jnp.where(((left >> k) & 1) == 1, 0, left))
    lane = lanes_iota((32, 128))
    out = jnp.zeros((32, 128), F32)
    for q, part in enumerate((first[0:32], first[32:64], second[0:32], second[32:64])):
        moved = part if q == 0 else pltpu.roll(part, 32 * q, 1)
        out = jnp.where((lane >> 5) == q, moved, out)
    return out


def unsqueeze(got, rank):
    parts = [got] + [pltpu.roll(got, 128 - 32 * q, 1) for q in (1, 2, 3)]
    first = jnp.concatenate(parts[0:2], axis=0)
    second = jnp.concatenate(parts[2:4], axis=0)
    index = jnp.minimum(rank, CAP - 1)
    out = []
    for m in range(8):
        for half in (first, second):
            out.append(
                jnp.take_along_axis(
                    half[8 * m : 8 * m + 8, :], index[8 * m : 8 * m + 8, :], axis=1, mode="promise_in_bounds"
                )
            )
    return jnp.concatenate(out, axis=0)


def send_body(p0, p1, w0, w1, gram, out, where, ranks):
    picks = jnp.concatenate([p0[...], p1[...]], axis=0)
    at = jnp.concatenate([w0[...], w1[...]], axis=0)
    where[...] = at
    live = halves_of(at)[0] >= 0
    before = (rows_iota((128, 128)) < lanes_iota((128, 128))).astype(F32).astype(BF)
    rank = dot(jnp.where(live, 1.0, 0.0).astype(BF), before, NN).astype(I32)
    ranks[...] = rank
    sent = squeeze(picks, live, rank).astype(BF)
    high = gram[...].astype(BF)
    low = (gram[...] - high.astype(F32)).astype(BF)
    for d in range(NY):
        out[d, 0:32, :] = sent
        out[d, 32:48, :] = high[16 * d : 16 * d + 16, :]
        out[d, 48:64, :] = low[16 * d : 16 * d + 16, :]


def resend_body(p0, p1, where, ranks, rows, out):
    picks = jnp.concatenate([p0[...], p1[...]], axis=0)
    live = halves_of(where[...])[0] >= 0
    sent = squeeze(picks, live, ranks[...]).astype(BF)
    for d in range(NY):
        out[d, 0:32, :] = sent
        out[d, 32:64, :] = rows[...]


def total(got, lo, hi):
    acc = got[0, lo:hi, :].astype(F32)
    for d in range(1, NY):
        acc = acc + got[d, lo:hi, :].astype(F32)
    return acc


def table_rows(at_t, val_t, m, half):
    lane = lanes_iota((R, 128))
    parts = []
    for q in range(4):
        k = 16 * m + 4 * half + q
        first = jnp.where(lane == at_t[:, k : k + 1], val_t[:, k : k + 1], 0.0)
        second = jnp.where(lane == at_t[:, k + 8 : k + 9], val_t[:, k + 8 : k + 9], 0.0)
        parts.append((first + second).astype(BF))
    return jnp.concatenate(parts, axis=1)


def decode(at_t, val_t, own, other, ms):
    halves = []
    for half, table in enumerate((own, other)):
        rows = [table_rows(at_t, val_t, m, half) for m in ms]
        rows = rows[0] if len(ms) == 1 else jnp.concatenate(rows, axis=0)
        halves.append(dot(rows, table[0 : 4 * R, :], NN))
    return halves[0] + halves[1]


def act_body(got, own, other, where, ranks, act, at_t, act_t, gram_rows, out):
    pre = unsqueeze(total(got, 0, 32), ranks[...])
    bias = []
    for table in (own, other):
        for q in range(4):
            ext = table[4 * R + 8 * q : 4 * R + 8 * q + 8, 0:384].astype(F32)
            bias.append((ext[0:1, 0:128] + ext[0:1, 128:256]) + ext[0:1, 256:384])
    bias = jnp.concatenate(bias, axis=0)
    at = where[...]
    shift = [
        jnp.take_along_axis(bias, jnp.maximum(at[8 * k : 8 * k + 8, :], 0), axis=1, mode="promise_in_bounds")
        for k in range(16)
    ]
    pre = pre + jnp.concatenate(shift, axis=0)
    value = jnp.where(at >= 0, pre.astype(BF).astype(F32), 0.0)
    act[...] = value
    turned = at.astype(F32).T.astype(I32)
    value_t = value.T
    at_t[...] = turned
    act_t[...] = value_t
    rows = total(got, 32, 48) + total(got, 48, 64)
    high = rows.astype(BF)
    gram_rows[0:16, :] = high
    gram_rows[16:32, :] = (rows - high.astype(F32)).astype(BF)
    out[...] = decode(turned, value_t, own, other, (7,)).astype(BF)


def decode_body(ms):
    def body(at_t, act_t, own, other, *outs):
        got = decode(at_t[...], act_t[...], own, other, ms)
        for i, out in enumerate(outs):
            out[...] = got[i * R : (i + 1) * R, :].astype(out.dtype)

    return body


def turned_table(at, val, b):
    atom = rows_iota((R, 128))
    parts = []
    for m in range(8):
        k = 16 * m + b
        first = jnp.where(atom == at[k : k + 1, :], val[k : k + 1, :], 0.0)
        second = jnp.where(atom == at[k + 8 : k + 9, :], val[k + 8 : k + 9, :], 0.0)
        parts.append(first + second)
    return parts


def load_rows(most, last, rows, sem):
    copies = [
        pltpu.make_async_copy(most, rows.at[pl.ds(0, 7 * R)], sem.at[0]),
        pltpu.make_async_copy(last.at[pl.ds(0, R)], rows.at[pl.ds(7 * R, R)], sem.at[1]),
    ]
    for copy in copies:
        copy.start()
    return copies


def tables_body(c0, c1, c2, c3, enc, dec):
    for i, ref in enumerate((c0, c1, c2, c3)):
        enc[R * i : R * (i + 1), :] = ref[0:R, :]
        dec[R * i : R * (i + 1), :] = ref[R : 2 * R, :]
        dec[4 * R + 8 * i : 4 * R + 8 * i + 8, :] = ref[2 * R : 2 * R + 8, :]


def fitted_body(half):
    def body(at, act, after, most, last, out, rows, sem):
        copies = load_rows(most, last, rows, sem)
        parts = [jnp.concatenate(turned_table(at, act, 4 * half + q), axis=1).astype(BF) for q in range(4)]
        table = jnp.concatenate(parts, axis=0)
        for copy in copies:
            copy.wait()
        out[...] = (dot(table, rows[...], NN) * LOSS_GRAD).astype(BF)

    return body


def encgrad_body(half):
    def body(got, at, ranks, most, last, *rest):
        out, (rows, sem) = rest[0], rest[-2:]
        copies = load_rows(most, last, rows, sem)
        grad = jnp.where(at[...] >= 0, unsqueeze(total(got, 0, 32), ranks[...]) * LOSS_GRAD, 0.0)
        if half == 0:
            gram = rest[1]
            for d in range(NY):
                gram[16 * d : 16 * d + 16, :] = got[d, 32:48, :].astype(F32) + got[d, 48:64, :].astype(F32)
        parts, ones = [], jnp.ones((8, 128), F32)
        for q in range(4):
            pieces = turned_table(at, grad, 4 * half + q)
            acc = pieces[0]
            for piece in pieces[1:]:
                acc = acc + piece
            sums = lax.dot_general(ones, acc, NT, precision=lax.Precision.HIGHEST, preferred_element_type=F32)
            out[q, R : R + 8, 0:128] = sums.astype(BF)
            out[q, R : R + 8, 128:1024] = jnp.zeros((8, 896), BF)
            parts.append(jnp.concatenate(pieces, axis=1).astype(BF))
        table = jnp.concatenate(parts, axis=0)
        for copy in copies:
            copy.wait()
        part = dot(table, rows[...], NN).astype(BF)
        for q in range(4):
            out[q, 0:R, :] = part[q * R : (q + 1) * R, :]

    return body


def penalty_body(count, gram_ref, decoder, out):
    gram = gram_ref[...]
    row, col = rows_iota((R, R)), lanes_iota((R, R))
    diagonal = row == col
    kept = jnp.where(diagonal, gram, 0.0)
    norm_c = jnp.sqrt(jnp.sum(kept, axis=1, keepdims=True) + EPSILON)
    norm_r = jnp.sqrt(jnp.sum(kept, axis=0, keepdims=True) + EPSILON)
    live = count[0] * BLOCK
    pair = norm_c * norm_r
    cosine = gram / pair
    alive = (row < live) & (col < live) & jnp.logical_not(diagonal)
    coupled = jnp.where(alive, cosine, 0.0)
    spread = jnp.sum(coupled * cosine, axis=1, keepdims=True)
    diag_term = jnp.where(diagonal, spread / (norm_c * norm_c), 0.0)
    weights = (4.0 * COHERENCE * (coupled / pair - diag_term)).astype(BF)
    out[...] = dot(weights, decoder[...], NN)


def finish_body(a, b, c, out, bias):
    total_of = lambda lo, hi, n: a[lo:hi, 0:n].astype(F32) + b[lo:hi, 0:n].astype(F32) + c[lo:hi, 0:n].astype(F32)
    out[...] = total_of(0, R, 1024).astype(BF)
    bias[...] = total_of(R, R + 8, R)


def add(a, b):
    return (a.astype(F32) + b.astype(F32)).astype(BF)


def gather_z(own):
    f1, b1 = move(own, dz=1), move(own, dz=-1)
    f2, b2 = move(f1, dz=1), move(b1, dz=-1)
    f3, b3 = move(f2, dz=1), move(b2, dz=-1)
    return [own, f1, b1, f2, b2, f3, b3, move(f3, dz=1)]


def scatter_x(own, theirs):
    blocks = [add(own[i], theirs[i]) for i in range(4)]
    far = move(blocks[3], dx=1)
    prev = move(blocks[1], dx=-1)
    return blocks[0], prev, move(add(blocks[2], far), dx=1)


def per_device(tokens, dec_bias, encoder, enc_bias, decoder, atom_ids, block_count):
    place = lax.axis_index("atoms")
    pos = jnp.stack([place >> 4, (place >> 1) & 7, place & 1]).astype(I32)
    bias_row = dec_bias.reshape(1, -1)

    sent = call(center_body, sds((R + 8, 1024), BF), tokens, bias_row, atom_ids, specs=whole(3))
    packed, gram_part = call(
        pack_body,
        (sds((2 * R + 8, 1024), BF), sds((R, R), F32)),
        encoder, decoder, enc_bias.reshape(1, -1), sent, specs=whole(3) + [ANY_SPEC],
    )
    tok = gather_z(sent)

    x1, x2 = move(packed, dx=1), move(packed, dx=-1)
    x3 = move(x1, dx=1)
    enc_own, dec_own = call(
        tables_body, (sds((4 * R, 1024), BF), sds((4 * R + 32, 1024), BF)), packed, x1, x2, x3,
        specs=whole(4),
    )
    enc_other = move(enc_own, dc=1)
    dec_other = move(dec_own, dc=1)

    def score(chunks):
        n = len(chunks)
        rows = [sds((n * R, 1024), BF)] if n > 1 else []
        return call(
            score_body(n),
            (sds((16 * n, 128), F32), sds((16 * n, 128), I32), *rows),
            pos, enc_own, enc_other, *chunks,
            specs=[SMEM_SPEC] + whole(2 + n),
        )

    pick_most, where_most, tok_most = score(tok[0:7])
    pick_last, where_last = score(tok[7:8])
    out, where, ranks = call(
        send_body, (sds((NY, 64, 128), BF), sds((R, R), I32), sds((64, R), I32)),
        pick_most, pick_last, where_most, where_last, gram_part, specs=whole(5),
    )
    got = lax.all_to_all(out, "width", split_axis=0, concat_axis=0, tiled=True)

    act, at_t, act_t, gram_rows, d7 = call(
        act_body,
        (sds((R, R), F32), sds((R, R), I32), sds((R, R), F32), sds((32, 128), BF), sds((R, 1024), BF)),
        got, dec_own, dec_other, where, ranks, specs=whole(5),
    )

    def decoded(ms, dtype=BF):
        return call(
            decode_body(ms), tuple(sds((R, 1024), dtype) for _ in ms),
            at_t, act_t, dec_own, dec_other, specs=whole(4),
        )

    d5, d6 = decoded((5, 6))
    d3, d4 = decoded((3, 4))
    d1, d2 = decoded((1, 2))
    (d0,) = decoded((0,), F32)
    f = move(d7, dz=1)
    b = move(d5, dz=-1)
    f = move(add(d6, f), dz=1)
    b = move(add(d3, b), dz=-1)
    f = move(add(d4, f), dz=1)
    b = move(add(d1, b), dz=-1)
    f = move(add(d2, f), dz=1)
    summed = d0 + f.astype(F32) + b.astype(F32)
    residual = (summed + bias_row - tokens.astype(F32)).astype(BF)

    res = gather_z(residual)

    def back(chunks, first):
        n = len(chunks)
        rows = [sds((n * R, 1024), BF)] if n > 1 else []
        return call(
            back_body(first, n), (sds((16 * n, 128), F32), *rows),
            dec_own, dec_other, where, *chunks, specs=whole(3 + n),
        )

    back_most, res_most = back(res[0:7], 0)
    (back_last,) = back(res[7:8], 7)
    out2 = call(resend_body, sds((NY, 64, 128), BF), back_most, back_last, where, ranks, gram_rows, specs=whole(5))
    got2 = lax.all_to_all(out2, "width", split_axis=0, concat_axis=0, tiled=True)

    scratch = [pltpu.VMEM((8 * R, 1024), BF), pltpu.SemaphoreType.DMA((2,))]

    def fitted(half, after):
        return call(
            fitted_body(half), sds((4 * R, 1024), BF), where, act, after, res_most, res[7],
            specs=whole(2) + [ANY_SPEC] * 3, scratch=scratch,
        )

    fit_other = fitted(1, out2)
    fit_theirs = move(fit_other, dc=1)
    fit_own = fitted(0, fit_other)
    fit = scatter_x(fit_own.reshape(4, R, 1024), fit_theirs.reshape(4, R, 1024))

    def encgrad(half):
        outs = [sds((4, R + 8, 1024), BF)] + ([sds((R, R), F32)] if half == 0 else [])
        return call(
            encgrad_body(half), tuple(outs), got2, where, ranks, tok_most, tok[7],
            specs=whole(3) + [ANY_SPEC] * 2, scratch=scratch,
        )

    (eg_other,) = encgrad(1)
    eg_theirs = move(eg_other, dc=1)
    eg_own, gram = encgrad(0)
    eg = scatter_x(eg_own, eg_theirs)
    encoder_grad, bias_grad = call(finish_body, (sds((R, 1024), BF), sds((8, R), F32)), *eg, specs=whole(3))
    bias_grad = bias_grad[0]

    penalty = call(penalty_body, sds((R, 1024), F32), block_count, gram, decoder, specs=[SMEM_SPEC] + whole(2))
    decoder_grad = (fit[0].astype(F32) + fit[1].astype(F32) + fit[2].astype(F32) + penalty).astype(BF)
    return (residual, encoder_grad, decoder_grad, bias_grad)


def solution(mesh):
    in_specs = (
        P("atoms", "width"),
        P("width"),
        P("atoms", "width"),
        P("atoms"),
        P("atoms", "width"),
        P("atoms", None),
        P("atoms"),
    )
    out_specs = (P("atoms", "width"), P("atoms", "width"), P("atoms", "width"), P("atoms"))
    return jax.shard_map(per_device, mesh=mesh, in_specs=in_specs, out_specs=out_specs, check_vma=False)
```

```python
import jax
import jax.numpy as jnp
from jax import lax
from jax.experimental import pallas as pl
from jax.experimental.pallas import tpu as pltpu
from jax.sharding import PartitionSpec as P


NX, NZ, NC, NY = 4, 8, 2, 8
BLOCK = 64
R = 128
COHERENCE = 128.0
LOSS_GRAD = 1.0 / 32.0
EPSILON = 1e-06
BF, F32, I32 = jnp.bfloat16, jnp.float32, jnp.int32
VMEM = 20 * 1024 * 1024
CAP = 24


def _place(x, z, c):
    return ((x % NX) * NZ + z % NZ) * NC + c % NC


def _perm(dx=0, dz=0, dc=0):
    return [
        (_place(x, z, c), _place(x + (dx if c == 0 else -dx), z + (dz if c == 0 else -dz), c + dc))
        for x in range(NX)
        for z in range(NZ)
        for c in range(NC)
    ]


def move(value, **shift):
    return lax.ppermute(value, "atoms", _perm(**shift))


def call(body, outs, *args, scratch=(), specs=None):
    return pl.pallas_call(
        body,
        out_shape=outs,
        in_specs=specs,
        scratch_shapes=scratch,
        compiler_params=pltpu.CompilerParams(vmem_limit_bytes=VMEM),
    )(*args)


def sds(shape, dtype):
    return jax.ShapeDtypeStruct(shape, dtype)


def whole(n):
    return [pl.BlockSpec(memory_space=pltpu.VMEM)] * n


SMEM_SPEC = pl.BlockSpec(memory_space=pltpu.SMEM)
ANY_SPEC = pl.BlockSpec(memory_space=pl.ANY)

NT = (((1,), (1,)), ((), ()))
NN = (((1,), (0,)), ((), ()))


def dot(a, b, dims):
    return lax.dot_general(a, b, dims, preferred_element_type=F32)


def rows_iota(shape):
    return lax.broadcasted_iota(I32, shape, 0)


def lanes_iota(shape):
    return lax.broadcasted_iota(I32, shape, 1)


def center_body(tokens, dec_bias, atom_ids, out):
    out[0:R, :] = (tokens[...].astype(F32) - dec_bias[...]).astype(BF)
    ids = atom_ids[...]
    owner = (ids >> 7).astype(F32).astype(BF)
    local = (ids & 127).astype(F32).astype(BF)
    row, col = rows_iota((8, 16)), lanes_iota((8, 16))
    even = (col == 2 * row).astype(F32).astype(BF)
    odd = (col == 2 * row + 1).astype(F32).astype(BF)
    out[R : R + 8, 0:128] = dot(even, owner, NT).astype(BF)
    out[R : R + 8, 128:256] = dot(even, local, NT).astype(BF)
    out[R : R + 8, 256:384] = dot(odd, local, NT).astype(BF)
    out[R : R + 8, 384:1024] = jnp.zeros((8, 640), BF)


def pack_body(encoder, decoder, enc_bias, after, out, gram):
    out[0:R, :] = encoder[...]
    out[R : 2 * R, :] = decoder[...]
    bias = jnp.broadcast_to(enc_bias[...], (8, 128))
    high = bias.astype(BF)
    rest = bias - high.astype(F32)
    mid = rest.astype(BF)
    low = (rest - mid.astype(F32)).astype(BF)
    out[2 * R : 2 * R + 8, 0:128] = high
    out[2 * R : 2 * R + 8, 128:256] = mid
    out[2 * R : 2 * R + 8, 256:384] = low
    out[2 * R : 2 * R + 8, 384:1024] = jnp.zeros((8, 640), BF)
    gram[...] = dot(decoder[...], decoder[...], NT)


def locate(ext, pos):
    x, z, c = pos[0], pos[1], pos[2]
    owner = ext[:, 0:128].astype(I32)
    first, second = ext[:, 128:256].astype(I32), ext[:, 256:384].astype(I32)
    dx = (((owner >> 4) - x) * (1 - 2 * (owner & 1)) + NX) & 3
    b = jnp.where(dx == 0, 0, jnp.where(dx == 3, 1, jnp.where(dx == 1, 2, 3)))
    b = b + jnp.where((owner & 1) == c, 0, 4)
    b = jnp.where(((owner >> 1) & 7) == z, b, -1)
    slot = rows_iota((8, 128))
    at_a = jnp.full((8, 128), -1, I32)
    at_b = jnp.full((8, 128), -1, I32)
    for g in range(8):
        hit = jnp.broadcast_to(b[g : g + 1, :], (8, 128)) == slot
        at_a = jnp.where(hit, jnp.broadcast_to(first[g : g + 1, :], (8, 128)), at_a)
        at_b = jnp.where(hit, jnp.broadcast_to(second[g : g + 1, :], (8, 128)), at_b)
    return at_a, at_b


def pick_into(out, tables, tok, places):
    n = len(places)
    atom = rows_iota((R, 128))
    for h, table in enumerate(tables):
        scores = dot(table[0 : 4 * R, :], tok, NT)
        for i in range(n):
            at_a, at_b = places[i]
            for q in range(4):
                b = 4 * h + q
                part = scores[q * R : (q + 1) * R, i * 128 : (i + 1) * 128]
                for s, at in ((0, at_a), (1, at_b)):
                    row = jnp.broadcast_to(at[b : b + 1, :], (R, 128))
                    got = jnp.sum(jnp.where(atom == row, part, 0.0), axis=0, keepdims=True)
                    out[16 * i + 8 * s + b : 16 * i + 8 * s + b + 1, :] = got


def score_some(pos, own, other, toks, exts, picks, where):
    places = [locate(ext, pos) for ext in exts]
    for i, (at_a, at_b) in enumerate(places):
        where[16 * i : 16 * i + 8, :] = at_a
        where[16 * i + 8 : 16 * i + 16, :] = at_b
    tok = toks[0] if len(toks) == 1 else jnp.concatenate(toks, axis=0)
    pick_into(picks, (own, other), tok, places)
    return tok


def score_body(pos, own, other, first, exts, t4, t5, t6, picks, where, rows):
    some = [exts[8 * i : 8 * i + 8, :] for i in range(4)] + [t[R : R + 8, 0:384].astype(F32) for t in (t4, t5, t6)]
    rows[...] = score_some(
        pos, own, other, [first[...]] + [t[0:R, :] for t in (t4, t5, t6)], some, picks, where
    )


def back_body(first, n):
    def body(own, other, where, *refs):
        chunks, (picks, *rows) = refs[:n], refs[n:]
        toks = [c[...] for c in chunks]
        places = []
        for i in range(n):
            at = 16 * (first + i)
            places.append((where[at : at + 8, :], where[at + 8 : at + 16, :]))
        tok = toks[0] if n == 1 else jnp.concatenate(toks, axis=0)
        for out in rows:
            out[...] = tok
        pick_into(picks, (own, other), tok, places)

    return body


def halves_of(packed):
    first = jnp.concatenate([packed[16 * m : 16 * m + 8, :] for m in range(8)], axis=0)
    second = jnp.concatenate([packed[16 * m + 8 : 16 * m + 16, :] for m in range(8)], axis=0)
    return first, second


def squeeze(picks, live, rank):
    first, second = halves_of(picks)
    lane = lanes_iota((64, 128))
    left = jnp.where(live, lane - rank, 0)
    for k in range(7):
        step = 128 - (1 << k)
        left_in = pltpu.roll(left, step, 1)
        hit = ((left_in >> k) & 1) == 1
        first = jnp.where(hit, pltpu.roll(first, step, 1), first)
        second = jnp.where(hit, pltpu.roll(second, step, 1), second)
        left = jnp.where(hit, left_in, jnp.where(((left >> k) & 1) == 1, 0, left))
    lane = lanes_iota((32, 128))
    out = jnp.zeros((32, 128), F32)
    for q, part in enumerate((first[0:32], first[32:64], second[0:32], second[32:64])):
        moved = part if q == 0 else pltpu.roll(part, 32 * q, 1)
        out = jnp.where((lane >> 5) == q, moved, out)
    return out


def unsqueeze(got, rank):
    parts = [got] + [pltpu.roll(got, 128 - 32 * q, 1) for q in (1, 2, 3)]
    first = jnp.concatenate(parts[0:2], axis=0)
    second = jnp.concatenate(parts[2:4], axis=0)
    index = jnp.minimum(rank, CAP - 1)
    out = []
    for m in range(8):
        for half in (first, second):
            out.append(
                jnp.take_along_axis(
                    half[8 * m : 8 * m + 8, :], index[8 * m : 8 * m + 8, :], axis=1, mode="promise_in_bounds"
                )
            )
    return jnp.concatenate(out, axis=0)


def send_body(pos, own, other, t7, p0, w0, gram, out, where, ranks, p1, w1):
    score_some(pos, own, other, [t7[0:R, :]], [t7[R : R + 8, 0:384].astype(F32)], p1, w1)
    picks = jnp.concatenate([p0[...], p1[...]], axis=0)
    at = jnp.concatenate([w0[...], w1[...]], axis=0)
    where[...] = at
    live = halves_of(at)[0] >= 0
    before = (rows_iota((128, 128)) < lanes_iota((128, 128))).astype(F32).astype(BF)
    rank = dot(jnp.where(live, 1.0, 0.0).astype(BF), before, NN).astype(I32)
    ranks[...] = rank
    sent = squeeze(picks, live, rank).astype(BF)
    high = gram[...].astype(BF)
    low = (gram[...] - high.astype(F32)).astype(BF)
    for d in range(NY):
        out[d, 0:32, :] = sent
        out[d, 32:48, :] = high[16 * d : 16 * d + 16, :]
        out[d, 48:64, :] = low[16 * d : 16 * d + 16, :]


def resend_body(p0, p1, where, ranks, rows, out):
    picks = jnp.concatenate([p0[...], p1[...]], axis=0)
    live = halves_of(where[...])[0] >= 0
    sent = squeeze(picks, live, ranks[...]).astype(BF)
    for d in range(NY):
        out[d, 0:32, :] = sent
        out[d, 32:64, :] = rows[...]


def total(got, lo, hi):
    acc = got[0, lo:hi, :].astype(F32)
    for d in range(1, NY):
        acc = acc + got[d, lo:hi, :].astype(F32)
    return acc


def table_rows(at_t, val_t, m, half):
    lane = lanes_iota((R, 128))
    parts = []
    for q in range(4):
        k = 16 * m + 4 * half + q
        first = jnp.where(lane == at_t[:, k : k + 1], val_t[:, k : k + 1], 0.0)
        second = jnp.where(lane == at_t[:, k + 8 : k + 9], val_t[:, k + 8 : k + 9], 0.0)
        parts.append((first + second).astype(BF))
    return jnp.concatenate(parts, axis=1)


def decode(at_t, val_t, own, other, ms):
    halves = []
    for half, table in enumerate((own, other)):
        rows = [table_rows(at_t, val_t, m, half) for m in ms]
        rows = rows[0] if len(ms) == 1 else jnp.concatenate(rows, axis=0)
        halves.append(dot(rows, table[0 : 4 * R, :], NN))
    return halves[0] + halves[1]


def act_body(got, own, other, where, ranks, act, at_t, act_t, gram_rows, out):
    pre = unsqueeze(total(got, 0, 32), ranks[...])
    bias = []
    for table in (own, other):
        for q in range(4):
            ext = table[4 * R + 8 * q : 4 * R + 8 * q + 8, 0:384].astype(F32)
            bias.append((ext[0:1, 0:128] + ext[0:1, 128:256]) + ext[0:1, 256:384])
    bias = jnp.concatenate(bias, axis=0)
    at = where[...]
    shift = [
        jnp.take_along_axis(bias, jnp.maximum(at[8 * k : 8 * k + 8, :], 0), axis=1, mode="promise_in_bounds")
        for k in range(16)
    ]
    pre = pre + jnp.concatenate(shift, axis=0)
    value = jnp.where(at >= 0, pre.astype(BF).astype(F32), 0.0)
    act[...] = value
    turned = at.astype(F32).T.astype(I32)
    value_t = value.T
    at_t[...] = turned
    act_t[...] = value_t
    rows = total(got, 32, 48) + total(got, 48, 64)
    high = rows.astype(BF)
    gram_rows[0:16, :] = high
    gram_rows[16:32, :] = (rows - high.astype(F32)).astype(BF)
    out[...] = decode(turned, value_t, own, other, (7,)).astype(BF)


def decode_body(ms):
    def body(at_t, act_t, own, other, *outs):
        got = decode(at_t[...], act_t[...], own, other, ms)
        for i, out in enumerate(outs):
            out[...] = got[i * R : (i + 1) * R, :].astype(out.dtype)

    return body


def turned_table(at, val, b):
    atom = rows_iota((R, 128))
    parts = []
    for m in range(8):
        k = 16 * m + b
        first = jnp.where(atom == at[k : k + 1, :], val[k : k + 1, :], 0.0)
        second = jnp.where(atom == at[k + 8 : k + 9, :], val[k + 8 : k + 9, :], 0.0)
        parts.append(first + second)
    return parts


def load_rows(most, last, rows, sem):
    copies = [
        pltpu.make_async_copy(most, rows.at[pl.ds(0, 7 * R)], sem.at[0]),
        pltpu.make_async_copy(last.at[pl.ds(0, R)], rows.at[pl.ds(7 * R, R)], sem.at[1]),
    ]
    for copy in copies:
        copy.start()
    return copies


def tables_body(c0, c1, c2, c3, t0, t1, t2, t3, enc, dec, rows, exts):
    for i, ref in enumerate((c0, c1, c2, c3)):
        enc[R * i : R * (i + 1), :] = ref[0:R, :]
        dec[R * i : R * (i + 1), :] = ref[R : 2 * R, :]
        dec[4 * R + 8 * i : 4 * R + 8 * i + 8, :] = ref[2 * R : 2 * R + 8, :]
    for i, ref in enumerate((t0, t1, t2, t3)):
        rows[R * i : R * (i + 1), :] = ref[0:R, :]
        exts[8 * i : 8 * i + 8, :] = ref[R : R + 8, 0:384].astype(F32)


def fitted_body(half):
    def body(at, act, after, most, last, out, rows, sem):
        copies = load_rows(most, last, rows, sem)
        parts = [jnp.concatenate(turned_table(at, act, 4 * half + q), axis=1).astype(BF) for q in range(4)]
        table = jnp.concatenate(parts, axis=0)
        for copy in copies:
            copy.wait()
        out[...] = (dot(table, rows[...], NN) * LOSS_GRAD).astype(BF)

    return body


def encgrad_body(half):
    def body(got, at, ranks, most, last, *rest):
        out, (rows, sem) = rest[0], rest[-2:]
        copies = load_rows(most, last, rows, sem)
        grad = jnp.where(at[...] >= 0, unsqueeze(total(got, 0, 32), ranks[...]) * LOSS_GRAD, 0.0)
        if half == 0:
            gram = rest[1]
            for d in range(NY):
                gram[16 * d : 16 * d + 16, :] = got[d, 32:48, :].astype(F32) + got[d, 48:64, :].astype(F32)
        parts, ones = [], jnp.ones((8, 128), F32)
        for q in range(4):
            pieces = turned_table(at, grad, 4 * half + q)
            acc = pieces[0]
            for piece in pieces[1:]:
                acc = acc + piece
            sums = lax.dot_general(ones, acc, NT, precision=lax.Precision.HIGHEST, preferred_element_type=F32)
            out[q, R : R + 8, 0:128] = sums.astype(BF)
            out[q, R : R + 8, 128:1024] = jnp.zeros((8, 896), BF)
            parts.append(jnp.concatenate(pieces, axis=1).astype(BF))
        table = jnp.concatenate(parts, axis=0)
        for copy in copies:
            copy.wait()
        part = dot(table, rows[...], NN).astype(BF)
        for q in range(4):
            out[q, 0:R, :] = part[q * R : (q + 1) * R, :]

    return body


def penalty_body(count, gram_ref, decoder, out):
    gram = gram_ref[...]
    row, col = rows_iota((R, R)), lanes_iota((R, R))
    diagonal = row == col
    kept = jnp.where(diagonal, gram, 0.0)
    norm_c = jnp.sqrt(jnp.sum(kept, axis=1, keepdims=True) + EPSILON)
    norm_r = jnp.sqrt(jnp.sum(kept, axis=0, keepdims=True) + EPSILON)
    live = count[0] * BLOCK
    pair = norm_c * norm_r
    cosine = gram / pair
    alive = (row < live) & (col < live) & jnp.logical_not(diagonal)
    coupled = jnp.where(alive, cosine, 0.0)
    spread = jnp.sum(coupled * cosine, axis=1, keepdims=True)
    diag_term = jnp.where(diagonal, spread / (norm_c * norm_c), 0.0)
    weights = (4.0 * COHERENCE * (coupled / pair - diag_term)).astype(BF)
    out[...] = dot(weights, decoder[...], NN)


def finish_body(a, b, c, out, bias):
    total_of = lambda lo, hi, n: a[lo:hi, 0:n].astype(F32) + b[lo:hi, 0:n].astype(F32) + c[lo:hi, 0:n].astype(F32)
    out[...] = total_of(0, R, 1024).astype(BF)
    bias[...] = total_of(R, R + 8, R)


def add(a, b):
    return (a.astype(F32) + b.astype(F32)).astype(BF)


def gather_z(own):
    f1, b1 = move(own, dz=1), move(own, dz=-1)
    f2, b2 = move(f1, dz=1), move(b1, dz=-1)
    f3, b3 = move(f2, dz=1), move(b2, dz=-1)
    return [own, f1, b1, f2, b2, f3, b3, move(f3, dz=1)]


def scatter_x(own, theirs):
    blocks = [add(own[i], theirs[i]) for i in range(4)]
    far = move(blocks[3], dx=1)
    prev = move(blocks[1], dx=-1)
    return blocks[0], prev, move(add(blocks[2], far), dx=1)


def per_device(tokens, dec_bias, encoder, enc_bias, decoder, atom_ids, block_count):
    place = lax.axis_index("atoms")
    pos = jnp.stack([place >> 4, (place >> 1) & 7, place & 1]).astype(I32)
    bias_row = dec_bias.reshape(1, -1)

    sent = call(center_body, sds((R + 8, 1024), BF), tokens, bias_row, atom_ids, specs=whole(3))
    packed, gram_part = call(
        pack_body,
        (sds((2 * R + 8, 1024), BF), sds((R, R), F32)),
        encoder, decoder, enc_bias.reshape(1, -1), sent, specs=whole(3) + [ANY_SPEC],
    )
    tok = gather_z(sent)

    x1, x2 = move(packed, dx=1), move(packed, dx=-1)
    x3 = move(x1, dx=1)
    enc_own, dec_own, tok_first, tok_exts = call(
        tables_body,
        (sds((4 * R, 1024), BF), sds((4 * R + 32, 1024), BF), sds((4 * R, 1024), BF), sds((32, 384), F32)),
        packed, x1, x2, x3, *tok[0:4], specs=whole(8),
    )
    enc_other = move(enc_own, dc=1)
    dec_other = move(dec_own, dc=1)

    pick_most, where_most, tok_most = call(
        score_body, (sds((112, 128), F32), sds((112, 128), I32), sds((7 * R, 1024), BF)),
        pos, enc_own, enc_other, tok_first, tok_exts, *tok[4:7], specs=[SMEM_SPEC] + whole(7),
    )
    out, where, ranks = call(
        send_body, (sds((NY, 64, 128), BF), sds((R, R), I32), sds((64, R), I32)),
        pos, enc_own, enc_other, tok[7], pick_most, where_most, gram_part, specs=[SMEM_SPEC] + whole(6),
        scratch=[pltpu.VMEM((16, 128), F32), pltpu.VMEM((16, 128), I32)],
    )
    got = lax.all_to_all(out, "width", split_axis=0, concat_axis=0, tiled=True)

    act, at_t, act_t, gram_rows, d7 = call(
        act_body,
        (sds((R, R), F32), sds((R, R), I32), sds((R, R), F32), sds((32, 128), BF), sds((R, 1024), BF)),
        got, dec_own, dec_other, where, ranks, specs=whole(5),
    )

    def decoded(ms, dtype=BF):
        return call(
            decode_body(ms), tuple(sds((R, 1024), dtype) for _ in ms),
            at_t, act_t, dec_own, dec_other, specs=whole(4),
        )

    d5, d6 = decoded((5, 6))
    d3, d4 = decoded((3, 4))
    d1, d2 = decoded((1, 2))
    (d0,) = decoded((0,), F32)
    f = move(d7, dz=1)
    b = move(d5, dz=-1)
    f = move(add(d6, f), dz=1)
    b = move(add(d3, b), dz=-1)
    f = move(add(d4, f), dz=1)
    b = move(add(d1, b), dz=-1)
    f = move(add(d2, f), dz=1)
    summed = d0 + f.astype(F32) + b.astype(F32)
    residual = (summed + bias_row - tokens.astype(F32)).astype(BF)

    res = gather_z(residual)

    def back(chunks, first):
        n = len(chunks)
        rows = [sds((n * R, 1024), BF)] if n > 1 else []
        return call(
            back_body(first, n), (sds((16 * n, 128), F32), *rows),
            dec_own, dec_other, where, *chunks, specs=whole(3 + n),
        )

    back_most, res_most = back(res[0:7], 0)
    (back_last,) = back(res[7:8], 7)
    out2 = call(resend_body, sds((NY, 64, 128), BF), back_most, back_last, where, ranks, gram_rows, specs=whole(5))
    got2 = lax.all_to_all(out2, "width", split_axis=0, concat_axis=0, tiled=True)

    scratch = [pltpu.VMEM((8 * R, 1024), BF), pltpu.SemaphoreType.DMA((2,))]

    def fitted(half, after):
        return call(
            fitted_body(half), sds((4 * R, 1024), BF), where, act, after, res_most, res[7],
            specs=whole(2) + [ANY_SPEC] * 3, scratch=scratch,
        )

    fit_other = fitted(1, out2)
    fit_theirs = move(fit_other, dc=1)
    fit_own = fitted(0, fit_other)
    fit = scatter_x(fit_own.reshape(4, R, 1024), fit_theirs.reshape(4, R, 1024))

    def encgrad(half):
        outs = [sds((4, R + 8, 1024), BF)] + ([sds((R, R), F32)] if half == 0 else [])
        return call(
            encgrad_body(half), tuple(outs), got2, where, ranks, tok_most, tok[7],
            specs=whole(3) + [ANY_SPEC] * 2, scratch=scratch,
        )

    (eg_other,) = encgrad(1)
    eg_theirs = move(eg_other, dc=1)
    eg_own, gram = encgrad(0)
    eg = scatter_x(eg_own, eg_theirs)
    encoder_grad, bias_grad = call(finish_body, (sds((R, 1024), BF), sds((8, R), F32)), *eg, specs=whole(3))
    bias_grad = bias_grad[0]

    penalty = call(penalty_body, sds((R, 1024), F32), block_count, gram, decoder, specs=[SMEM_SPEC] + whole(2))
    decoder_grad = (fit[0].astype(F32) + fit[1].astype(F32) + fit[2].astype(F32) + penalty).astype(BF)
    return (residual, encoder_grad, decoder_grad, bias_grad)


def solution(mesh):
    in_specs = (
        P("atoms", "width"),
        P("width"),
        P("atoms", "width"),
        P("atoms"),
        P("atoms", "width"),
        P("atoms", None),
        P("atoms"),
    )
    out_specs = (P("atoms", "width"), P("atoms", "width"), P("atoms", "width"), P("atoms"))
    return jax.shard_map(per_device, mesh=mesh, in_specs=in_specs, out_specs=out_specs, check_vma=False)
```

```python
import jax
import jax.numpy as jnp
from jax import lax
from jax.experimental import pallas as pl
from jax.experimental.pallas import tpu as pltpu
from jax.sharding import PartitionSpec as P


NX, NZ, NC, NY = 4, 8, 2, 8
BLOCK = 64
R = 128
COHERENCE = 128.0
LOSS_GRAD = 1.0 / 32.0
EPSILON = 1e-06
BF, F32, I32 = jnp.bfloat16, jnp.float32, jnp.int32
VMEM = 20 * 1024 * 1024
CAP = 24


def _place(x, z, c):
    return ((x % NX) * NZ + z % NZ) * NC + c % NC


def _perm(dx=0, dz=0, dc=0):
    return [
        (_place(x, z, c), _place(x + (dx if c == 0 else -dx), z + (dz if c == 0 else -dz), c + dc))
        for x in range(NX)
        for z in range(NZ)
        for c in range(NC)
    ]


def move(value, **shift):
    return lax.ppermute(value, "atoms", _perm(**shift))


def call(body, outs, *args, scratch=(), specs=None):
    return pl.pallas_call(
        body,
        out_shape=outs,
        in_specs=specs,
        scratch_shapes=scratch,
        compiler_params=pltpu.CompilerParams(vmem_limit_bytes=VMEM),
    )(*args)


def sds(shape, dtype):
    return jax.ShapeDtypeStruct(shape, dtype)


def whole(n):
    return [pl.BlockSpec(memory_space=pltpu.VMEM)] * n


SMEM_SPEC = pl.BlockSpec(memory_space=pltpu.SMEM)
ANY_SPEC = pl.BlockSpec(memory_space=pl.ANY)

NT = (((1,), (1,)), ((), ()))
NN = (((1,), (0,)), ((), ()))


def dot(a, b, dims):
    return lax.dot_general(a, b, dims, preferred_element_type=F32)


def rows_iota(shape):
    return lax.broadcasted_iota(I32, shape, 0)


def lanes_iota(shape):
    return lax.broadcasted_iota(I32, shape, 1)


def center_body(tokens, dec_bias, atom_ids, out):
    out[0:R, :] = (tokens[...].astype(F32) - dec_bias[...]).astype(BF)
    ids = atom_ids[...]
    owner = (ids >> 7).astype(F32).astype(BF)
    local = (ids & 127).astype(F32).astype(BF)
    row, col = rows_iota((8, 16)), lanes_iota((8, 16))
    even = (col == 2 * row).astype(F32).astype(BF)
    odd = (col == 2 * row + 1).astype(F32).astype(BF)
    out[R : R + 8, 0:128] = dot(even, owner, NT).astype(BF)
    out[R : R + 8, 128:256] = dot(even, local, NT).astype(BF)
    out[R : R + 8, 256:384] = dot(odd, local, NT).astype(BF)
    out[R : R + 8, 384:1024] = jnp.zeros((8, 640), BF)


def pack_body(encoder, decoder, enc_bias, after, out, gram):
    out[0:R, :] = encoder[...]
    out[R : 2 * R, :] = decoder[...]
    bias = jnp.broadcast_to(enc_bias[...], (8, 128))
    high = bias.astype(BF)
    rest = bias - high.astype(F32)
    mid = rest.astype(BF)
    low = (rest - mid.astype(F32)).astype(BF)
    out[2 * R : 2 * R + 8, 0:128] = high
    out[2 * R : 2 * R + 8, 128:256] = mid
    out[2 * R : 2 * R + 8, 256:384] = low
    out[2 * R : 2 * R + 8, 384:1024] = jnp.zeros((8, 640), BF)
    gram[...] = dot(decoder[...], decoder[...], NT)


def locate(ext, pos):
    x, z, c = pos[0], pos[1], pos[2]
    owner = ext[:, 0:128].astype(I32)
    first, second = ext[:, 128:256].astype(I32), ext[:, 256:384].astype(I32)
    dx = (((owner >> 4) - x) * (1 - 2 * (owner & 1)) + NX) & 3
    b = jnp.where(dx == 0, 0, jnp.where(dx == 3, 1, jnp.where(dx == 1, 2, 3)))
    b = b + jnp.where((owner & 1) == c, 0, 4)
    b = jnp.where(((owner >> 1) & 7) == z, b, -1)
    slot = rows_iota((8, 128))
    at_a = jnp.full((8, 128), -1, I32)
    at_b = jnp.full((8, 128), -1, I32)
    for g in range(8):
        hit = jnp.broadcast_to(b[g : g + 1, :], (8, 128)) == slot
        at_a = jnp.where(hit, jnp.broadcast_to(first[g : g + 1, :], (8, 128)), at_a)
        at_b = jnp.where(hit, jnp.broadcast_to(second[g : g + 1, :], (8, 128)), at_b)
    return at_a, at_b


def pick_into(out, tables, tok, places):
    n = len(places)
    atom = rows_iota((R, 128))
    for h, table in enumerate(tables):
        scores = dot(table[0 : 4 * R, :], tok, NT)
        for i in range(n):
            at_a, at_b = places[i]
            for q in range(4):
                b = 4 * h + q
                part = scores[q * R : (q + 1) * R, i * 128 : (i + 1) * 128]
                for s, at in ((0, at_a), (1, at_b)):
                    row = jnp.broadcast_to(at[b : b + 1, :], (R, 128))
                    got = jnp.sum(jnp.where(atom == row, part, 0.0), axis=0, keepdims=True)
                    out[16 * i + 8 * s + b : 16 * i + 8 * s + b + 1, :] = got


def score_some(pos, own, other, toks, exts, picks, where):
    places = [locate(ext, pos) for ext in exts]
    for i, (at_a, at_b) in enumerate(places):
        where[16 * i : 16 * i + 8, :] = at_a
        where[16 * i + 8 : 16 * i + 16, :] = at_b
    tok = toks[0] if len(toks) == 1 else jnp.concatenate(toks, axis=0)
    pick_into(picks, (own, other), tok, places)
    return tok


def score_body(pos, own, other, first, exts, t4, t5, t6, picks, where, rows):
    some = [exts[8 * i : 8 * i + 8, :] for i in range(4)] + [t[R : R + 8, 0:384].astype(F32) for t in (t4, t5, t6)]
    rows[...] = score_some(
        pos, own, other, [first[...]] + [t[0:R, :] for t in (t4, t5, t6)], some, picks, where
    )


def back_body(own, other, where, *refs):
    chunks, (picks, rows) = refs[:7], refs[7:]
    places = [(where[16 * i : 16 * i + 8, :], where[16 * i + 8 : 16 * i + 16, :]) for i in range(7)]
    tok = jnp.concatenate([c[...] for c in chunks], axis=0)
    rows[...] = tok
    pick_into(picks, (own, other), tok, places)


def halves_of(packed):
    first = jnp.concatenate([packed[16 * m : 16 * m + 8, :] for m in range(8)], axis=0)
    second = jnp.concatenate([packed[16 * m + 8 : 16 * m + 16, :] for m in range(8)], axis=0)
    return first, second


def squeeze(picks, live, rank):
    first, second = halves_of(picks)
    lane = lanes_iota((64, 128))
    left = jnp.where(live, lane - rank, 0)
    for k in range(7):
        step = 128 - (1 << k)
        left_in = pltpu.roll(left, step, 1)
        hit = ((left_in >> k) & 1) == 1
        first = jnp.where(hit, pltpu.roll(first, step, 1), first)
        second = jnp.where(hit, pltpu.roll(second, step, 1), second)
        left = jnp.where(hit, left_in, jnp.where(((left >> k) & 1) == 1, 0, left))
    lane = lanes_iota((32, 128))
    out = jnp.zeros((32, 128), F32)
    for q, part in enumerate((first[0:32], first[32:64], second[0:32], second[32:64])):
        moved = part if q == 0 else pltpu.roll(part, 32 * q, 1)
        out = jnp.where((lane >> 5) == q, moved, out)
    return out


def unsqueeze(got, rank):
    parts = [got] + [pltpu.roll(got, 128 - 32 * q, 1) for q in (1, 2, 3)]
    first = jnp.concatenate(parts[0:2], axis=0)
    second = jnp.concatenate(parts[2:4], axis=0)
    index = jnp.minimum(rank, CAP - 1)
    out = []
    for m in range(8):
        for half in (first, second):
            out.append(
                jnp.take_along_axis(
                    half[8 * m : 8 * m + 8, :], index[8 * m : 8 * m + 8, :], axis=1, mode="promise_in_bounds"
                )
            )
    return jnp.concatenate(out, axis=0)


def send_body(pos, own, other, t7, p0, w0, gram, out, where, ranks, p1, w1):
    score_some(pos, own, other, [t7[0:R, :]], [t7[R : R + 8, 0:384].astype(F32)], p1, w1)
    picks = jnp.concatenate([p0[...], p1[...]], axis=0)
    at = jnp.concatenate([w0[...], w1[...]], axis=0)
    where[...] = at
    live = halves_of(at)[0] >= 0
    before = (rows_iota((128, 128)) < lanes_iota((128, 128))).astype(F32).astype(BF)
    rank = dot(jnp.where(live, 1.0, 0.0).astype(BF), before, NN).astype(I32)
    ranks[...] = rank
    sent = squeeze(picks, live, rank).astype(BF)
    high = gram[...].astype(BF)
    low = (gram[...] - high.astype(F32)).astype(BF)
    for d in range(NY):
        out[d, 0:32, :] = sent
        out[d, 32:48, :] = high[16 * d : 16 * d + 16, :]
        out[d, 48:64, :] = low[16 * d : 16 * d + 16, :]


def resend_body(own, other, where, t7, p0, ranks, rows, out, p1):
    pick_into(p1, (own, other), t7[...], [(where[112:120, :], where[120:128, :])])
    picks = jnp.concatenate([p0[...], p1[...]], axis=0)
    live = halves_of(where[...])[0] >= 0
    sent = squeeze(picks, live, ranks[...]).astype(BF)
    for d in range(NY):
        out[d, 0:32, :] = sent
        out[d, 32:64, :] = rows[...]


def total(got, lo, hi):
    acc = got[0, lo:hi, :].astype(F32)
    for d in range(1, NY):
        acc = acc + got[d, lo:hi, :].astype(F32)
    return acc


def table_rows(at_t, val_t, m, half):
    lane = lanes_iota((R, 128))
    parts = []
    for q in range(4):
        k = 16 * m + 4 * half + q
        first = jnp.where(lane == at_t[:, k : k + 1], val_t[:, k : k + 1], 0.0)
        second = jnp.where(lane == at_t[:, k + 8 : k + 9], val_t[:, k + 8 : k + 9], 0.0)
        parts.append((first + second).astype(BF))
    return jnp.concatenate(parts, axis=1)


def decode(at_t, val_t, own, other, ms):
    halves = []
    for half, table in enumerate((own, other)):
        rows = [table_rows(at_t, val_t, m, half) for m in ms]
        rows = rows[0] if len(ms) == 1 else jnp.concatenate(rows, axis=0)
        halves.append(dot(rows, table[0 : 4 * R, :], NN))
    return halves[0] + halves[1]


def act_body(got, own, other, where, ranks, act, at_t, act_t, gram_rows, out):
    pre = unsqueeze(total(got, 0, 32), ranks[...])
    bias = []
    for table in (own, other):
        for q in range(4):
            ext = table[4 * R + 8 * q : 4 * R + 8 * q + 8, 0:384].astype(F32)
            bias.append((ext[0:1, 0:128] + ext[0:1, 128:256]) + ext[0:1, 256:384])
    bias = jnp.concatenate(bias, axis=0)
    at = where[...]
    shift = [
        jnp.take_along_axis(bias, jnp.maximum(at[8 * k : 8 * k + 8, :], 0), axis=1, mode="promise_in_bounds")
        for k in range(16)
    ]
    pre = pre + jnp.concatenate(shift, axis=0)
    value = jnp.where(at >= 0, pre.astype(BF).astype(F32), 0.0)
    act[...] = value
    turned = at.astype(F32).T.astype(I32)
    value_t = value.T
    at_t[...] = turned
    act_t[...] = value_t
    rows = total(got, 32, 48) + total(got, 48, 64)
    high = rows.astype(BF)
    gram_rows[0:16, :] = high
    gram_rows[16:32, :] = (rows - high.astype(F32)).astype(BF)
    out[...] = decode(turned, value_t, own, other, (7,)).astype(BF)


def decode_body(ms):
    def body(at_t, act_t, own, other, *outs):
        got = decode(at_t[...], act_t[...], own, other, ms)
        for i, out in enumerate(outs):
            out[...] = got[i * R : (i + 1) * R, :].astype(out.dtype)

    return body


def turned_table(at, val, b):
    atom = rows_iota((R, 128))
    parts = []
    for m in range(8):
        k = 16 * m + b
        first = jnp.where(atom == at[k : k + 1, :], val[k : k + 1, :], 0.0)
        second = jnp.where(atom == at[k + 8 : k + 9, :], val[k + 8 : k + 9, :], 0.0)
        parts.append(first + second)
    return parts


def load_rows(most, last, rows, sem):
    copies = [
        pltpu.make_async_copy(most, rows.at[pl.ds(0, 7 * R)], sem.at[0]),
        pltpu.make_async_copy(last.at[pl.ds(0, R)], rows.at[pl.ds(7 * R, R)], sem.at[1]),
    ]
    for copy in copies:
        copy.start()
    return copies


def tables_body(c0, c1, c2, c3, t0, t1, t2, t3, enc, dec, rows, exts):
    for i, ref in enumerate((c0, c1, c2, c3)):
        enc[R * i : R * (i + 1), :] = ref[0:R, :]
        dec[R * i : R * (i + 1), :] = ref[R : 2 * R, :]
        dec[4 * R + 8 * i : 4 * R + 8 * i + 8, :] = ref[2 * R : 2 * R + 8, :]
    for i, ref in enumerate((t0, t1, t2, t3)):
        rows[R * i : R * (i + 1), :] = ref[0:R, :]
        exts[8 * i : 8 * i + 8, :] = ref[R : R + 8, 0:384].astype(F32)


def x_slot(pos, q, half):
    side = 1 - 2 * pos[2] if half == 0 else 2 * pos[2] - 1
    return (pos[0] + (0, -side, side, 2)[q] + NX) & 3


def fitted_body(half):
    def body(at, act, after, most, last, out, rows, sem):
        copies = load_rows(most, last, rows, sem)
        parts = [jnp.concatenate(turned_table(at, act, 4 * half + q), axis=1).astype(BF) for q in range(4)]
        table = jnp.concatenate(parts, axis=0)
        for copy in copies:
            copy.wait()
        part = (dot(table, rows[...], NN) * LOSS_GRAD).astype(BF)
        for q in range(4):
            out[q] = part[q * R : (q + 1) * R, :]

    return body


def encgrad_body(half):
    def body(pos, got, at, ranks, most, last, *rest):
        out, (rows, sem) = rest[0], rest[-2:]
        copies = load_rows(most, last, rows, sem)
        grad = jnp.where(at[...] >= 0, unsqueeze(total(got, 0, 32), ranks[...]) * LOSS_GRAD, 0.0)
        if half == 0:
            gram = rest[1]
            for d in range(NY):
                gram[16 * d : 16 * d + 16, :] = got[d, 32:48, :].astype(F32) + got[d, 48:64, :].astype(F32)
        parts, ones = [], jnp.ones((8, 128), F32)
        for q in range(4):
            pieces = turned_table(at, grad, 4 * half + q)
            acc = pieces[0]
            for piece in pieces[1:]:
                acc = acc + piece
            sums = lax.dot_general(ones, acc, NT, precision=lax.Precision.HIGHEST, preferred_element_type=F32)
            slot = x_slot(pos, q, half)
            out[slot, R : R + 8, 0:128] = sums.astype(BF)
            out[slot, R : R + 8, 128:1024] = jnp.zeros((8, 896), BF)
            parts.append(jnp.concatenate(pieces, axis=1).astype(BF))
        table = jnp.concatenate(parts, axis=0)
        for copy in copies:
            copy.wait()
        part = dot(table, rows[...], NN).astype(BF)
        for q in range(4):
            out[x_slot(pos, q, half), 0:R, :] = part[q * R : (q + 1) * R, :]

    return body


def penalty_body(count, gram_ref, decoder, a, b, c, out):
    gram = gram_ref[...]
    row, col = rows_iota((R, R)), lanes_iota((R, R))
    diagonal = row == col
    kept = jnp.where(diagonal, gram, 0.0)
    norm_c = jnp.sqrt(jnp.sum(kept, axis=1, keepdims=True) + EPSILON)
    norm_r = jnp.sqrt(jnp.sum(kept, axis=0, keepdims=True) + EPSILON)
    live = count[0] * BLOCK
    pair = norm_c * norm_r
    cosine = gram / pair
    alive = (row < live) & (col < live) & jnp.logical_not(diagonal)
    coupled = jnp.where(alive, cosine, 0.0)
    spread = jnp.sum(coupled * cosine, axis=1, keepdims=True)
    diag_term = jnp.where(diagonal, spread / (norm_c * norm_c), 0.0)
    weights = (4.0 * COHERENCE * (coupled / pair - diag_term)).astype(BF)
    fit = (a[...].astype(F32) + b[...].astype(F32)) + c[...].astype(F32)
    out[...] = (fit + dot(weights, decoder[...], NN)).astype(BF)


def sum_of(got, lo, hi, n):
    acc = got[0, lo:hi, 0:n].astype(F32)
    for i in range(1, NX):
        acc = acc + got[i, lo:hi, 0:n].astype(F32)
    return acc


def finish_body(got, out, bias):
    out[...] = sum_of(got, 0, R, 1024).astype(BF)
    bias[...] = sum_of(got, R, R + 8, R)


def add(a, b):
    return (a.astype(F32) + b.astype(F32)).astype(BF)


def gather_z(own):
    f1, b1 = move(own, dz=1), move(own, dz=-1)
    f2, b2 = move(f1, dz=1), move(b1, dz=-1)
    f3, b3 = move(f2, dz=1), move(b2, dz=-1)
    return [own, f1, b1, f2, b2, f3, b3, move(f3, dz=1)]


def ring_x(own, theirs):
    blocks = [add(own[i], theirs[i]) for i in range(4)]
    far = move(blocks[3], dx=1)
    prev = move(blocks[1], dx=-1)
    return blocks[0], prev, move(add(blocks[2], far), dx=1)


def scatter_x(own, theirs):
    groups = [[_place(x, z, c) for x in range(NX)] for z in range(NZ) for c in range(NC)]
    return lax.all_to_all(add(own, theirs), "atoms", split_axis=0, concat_axis=0, tiled=True, axis_index_groups=groups)


def per_device(tokens, dec_bias, encoder, enc_bias, decoder, atom_ids, block_count):
    place = lax.axis_index("atoms")
    pos = jnp.stack([place >> 4, (place >> 1) & 7, place & 1]).astype(I32)
    bias_row = dec_bias.reshape(1, -1)

    sent = call(center_body, sds((R + 8, 1024), BF), tokens, bias_row, atom_ids, specs=whole(3))
    packed, gram_part = call(
        pack_body,
        (sds((2 * R + 8, 1024), BF), sds((R, R), F32)),
        encoder, decoder, enc_bias.reshape(1, -1), sent, specs=whole(3) + [ANY_SPEC],
    )
    tok = gather_z(sent)

    x1, x2 = move(packed, dx=1), move(packed, dx=-1)
    x3 = move(x1, dx=1)
    enc_own, dec_own, tok_first, tok_exts = call(
        tables_body,
        (sds((4 * R, 1024), BF), sds((4 * R + 32, 1024), BF), sds((4 * R, 1024), BF), sds((32, 384), F32)),
        packed, x1, x2, x3, *tok[0:4], specs=whole(8),
    )
    enc_other = move(enc_own, dc=1)
    dec_other = move(dec_own, dc=1)

    pick_most, where_most, tok_most = call(
        score_body, (sds((112, 128), F32), sds((112, 128), I32), sds((7 * R, 1024), BF)),
        pos, enc_own, enc_other, tok_first, tok_exts, *tok[4:7], specs=[SMEM_SPEC] + whole(7),
    )
    out, where, ranks = call(
        send_body, (sds((NY, 64, 128), BF), sds((R, R), I32), sds((64, R), I32)),
        pos, enc_own, enc_other, tok[7], pick_most, where_most, gram_part, specs=[SMEM_SPEC] + whole(6),
        scratch=[pltpu.VMEM((16, 128), F32), pltpu.VMEM((16, 128), I32)],
    )
    got = lax.all_to_all(out, "width", split_axis=0, concat_axis=0, tiled=True)

    act, at_t, act_t, gram_rows, d7 = call(
        act_body,
        (sds((R, R), F32), sds((R, R), I32), sds((R, R), F32), sds((32, 128), BF), sds((R, 1024), BF)),
        got, dec_own, dec_other, where, ranks, specs=whole(5),
    )

    def decoded(ms, dtype=BF):
        return call(
            decode_body(ms), tuple(sds((R, 1024), dtype) for _ in ms),
            at_t, act_t, dec_own, dec_other, specs=whole(4),
        )

    d5, d6 = decoded((5, 6))
    d3, d4 = decoded((3, 4))
    d1, d2 = decoded((1, 2))
    (d0,) = decoded((0,), F32)
    f = move(d7, dz=1)
    b = move(d5, dz=-1)
    f = move(add(d6, f), dz=1)
    b = move(add(d3, b), dz=-1)
    f = move(add(d4, f), dz=1)
    b = move(add(d1, b), dz=-1)
    f = move(add(d2, f), dz=1)
    summed = d0 + f.astype(F32) + b.astype(F32)
    residual = (summed + bias_row - tokens.astype(F32)).astype(BF)

    res = gather_z(residual)

    back_most, res_most = call(
        back_body, (sds((112, 128), F32), sds((7 * R, 1024), BF)), dec_own, dec_other, where, *res[0:7],
        specs=whole(10),
    )
    out2 = call(
        resend_body, sds((NY, 64, 128), BF), dec_own, dec_other, where, res[7], back_most, ranks, gram_rows,
        specs=whole(7), scratch=[pltpu.VMEM((16, 128), F32)],
    )
    got2 = lax.all_to_all(out2, "width", split_axis=0, concat_axis=0, tiled=True)

    scratch = [pltpu.VMEM((8 * R, 1024), BF), pltpu.SemaphoreType.DMA((2,))]

    def fitted(half, after):
        return call(
            fitted_body(half), sds((4, R, 1024), BF), where, act, after, res_most, res[7],
            specs=whole(2) + [ANY_SPEC] * 3, scratch=scratch,
        )

    fit_other = fitted(1, out2)
    fit_theirs = move(fit_other, dc=1)
    fit_own = fitted(0, fit_other)
    fit = ring_x(fit_own, fit_theirs)

    def encgrad(half):
        outs = [sds((4, R + 8, 1024), BF)] + ([sds((R, R), F32)] if half == 0 else [])
        return call(
            encgrad_body(half), tuple(outs), pos, got2, where, ranks, tok_most, tok[7],
            specs=[SMEM_SPEC] + whole(3) + [ANY_SPEC] * 2, scratch=scratch,
        )

    (eg_other,) = encgrad(1)
    eg_theirs = move(eg_other, dc=1)
    eg_own, gram = encgrad(0)
    eg = scatter_x(eg_own, eg_theirs)
    encoder_grad, bias_grad = call(finish_body, (sds((R, 1024), BF), sds((8, R), F32)), eg, specs=whole(1))
    bias_grad = bias_grad[0]

    decoder_grad = call(
        penalty_body, sds((R, 1024), BF), block_count, gram, decoder, *fit, specs=[SMEM_SPEC] + whole(5)
    )
    return (residual, encoder_grad, decoder_grad, bias_grad)


def solution(mesh):
    in_specs = (
        P("atoms", "width"),
        P("width"),
        P("atoms", "width"),
        P("atoms"),
        P("atoms", "width"),
        P("atoms", None),
        P("atoms"),
    )
    out_specs = (P("atoms", "width"), P("atoms", "width"), P("atoms", "width"), P("atoms"))
    return jax.shard_map(per_device, mesh=mesh, in_specs=in_specs, out_specs=out_specs, check_vma=False)
```

```python
import jax
import jax.numpy as jnp
from jax import lax
from jax.experimental import pallas as pl
from jax.experimental.pallas import tpu as pltpu
from jax.sharding import PartitionSpec as P


NX, NZ, NC, NY = 4, 8, 2, 8
BLOCK = 64
R = 128
COHERENCE = 128.0
LOSS_GRAD = 1.0 / 32.0
EPSILON = 1e-06
BF, F32, I32 = jnp.bfloat16, jnp.float32, jnp.int32
VMEM = 20 * 1024 * 1024
CAP = 24


def _place(x, z, c):
    return ((x % NX) * NZ + z % NZ) * NC + c % NC


def _perm(dx=0, dz=0, dc=0):
    return [
        (_place(x, z, c), _place(x + (dx if c == 0 else -dx), z + (dz if c == 0 else -dz), c + dc))
        for x in range(NX)
        for z in range(NZ)
        for c in range(NC)
    ]


def move(value, **shift):
    return lax.ppermute(value, "atoms", _perm(**shift))


def call(body, outs, *args, scratch=(), specs=None):
    return pl.pallas_call(
        body,
        out_shape=outs,
        in_specs=specs,
        scratch_shapes=scratch,
        compiler_params=pltpu.CompilerParams(vmem_limit_bytes=VMEM),
    )(*args)


def sds(shape, dtype):
    return jax.ShapeDtypeStruct(shape, dtype)


def whole(n):
    return [pl.BlockSpec(memory_space=pltpu.VMEM)] * n


SMEM_SPEC = pl.BlockSpec(memory_space=pltpu.SMEM)
ANY_SPEC = pl.BlockSpec(memory_space=pl.ANY)

NT = (((1,), (1,)), ((), ()))
NN = (((1,), (0,)), ((), ()))


def dot(a, b, dims):
    return lax.dot_general(a, b, dims, preferred_element_type=F32)


def rows_iota(shape):
    return lax.broadcasted_iota(I32, shape, 0)


def lanes_iota(shape):
    return lax.broadcasted_iota(I32, shape, 1)


def center_body(tokens, dec_bias, atom_ids, out):
    out[0:R, :] = (tokens[...].astype(F32) - dec_bias[...]).astype(BF)
    ids = atom_ids[...]
    owner = (ids >> 7).astype(F32).astype(BF)
    local = (ids & 127).astype(F32).astype(BF)
    row, col = rows_iota((8, 16)), lanes_iota((8, 16))
    even = (col == 2 * row).astype(F32).astype(BF)
    odd = (col == 2 * row + 1).astype(F32).astype(BF)
    out[R : R + 8, 0:128] = dot(even, owner, NT).astype(BF)
    out[R : R + 8, 128:256] = dot(even, local, NT).astype(BF)
    out[R : R + 8, 256:384] = dot(odd, local, NT).astype(BF)
    out[R : R + 8, 384:1024] = jnp.zeros((8, 640), BF)


def pack_body(encoder, decoder, enc_bias, after, out, gram):
    out[0:R, :] = encoder[...]
    out[R : 2 * R, :] = decoder[...]
    bias = jnp.broadcast_to(enc_bias[...], (8, 128))
    high = bias.astype(BF)
    rest = bias - high.astype(F32)
    mid = rest.astype(BF)
    low = (rest - mid.astype(F32)).astype(BF)
    out[2 * R : 2 * R + 8, 0:128] = high
    out[2 * R : 2 * R + 8, 128:256] = mid
    out[2 * R : 2 * R + 8, 256:384] = low
    out[2 * R : 2 * R + 8, 384:1024] = jnp.zeros((8, 640), BF)
    gram[...] = dot(decoder[...], decoder[...], NT)


def locate(ext, pos):
    x, z, c = pos[0], pos[1], pos[2]
    owner = ext[:, 0:128].astype(I32)
    first, second = ext[:, 128:256].astype(I32), ext[:, 256:384].astype(I32)
    dx = (((owner >> 4) - x) * (1 - 2 * (owner & 1)) + NX) & 3
    b = jnp.where(dx == 0, 0, jnp.where(dx == 3, 1, jnp.where(dx == 1, 2, 3)))
    b = b + jnp.where((owner & 1) == c, 0, 4)
    b = jnp.where(((owner >> 1) & 7) == z, b, -1)
    slot = rows_iota((8, 128))
    at_a = jnp.full((8, 128), -1, I32)
    at_b = jnp.full((8, 128), -1, I32)
    for g in range(8):
        hit = jnp.broadcast_to(b[g : g + 1, :], (8, 128)) == slot
        at_a = jnp.where(hit, jnp.broadcast_to(first[g : g + 1, :], (8, 128)), at_a)
        at_b = jnp.where(hit, jnp.broadcast_to(second[g : g + 1, :], (8, 128)), at_b)
    return at_a, at_b


def pick_into(out, tables, tok, places):
    n = len(places)
    atom = rows_iota((R, 128))
    for h, table in enumerate(tables):
        scores = dot(table[0 : 4 * R, :], tok, NT)
        for i in range(n):
            at_a, at_b = places[i]
            for q in range(4):
                b = 4 * h + q
                part = scores[q * R : (q + 1) * R, i * 128 : (i + 1) * 128]
                for s, at in ((0, at_a), (1, at_b)):
                    row = jnp.broadcast_to(at[b : b + 1, :], (R, 128))
                    got = jnp.sum(jnp.where(atom == row, part, 0.0), axis=0, keepdims=True)
                    out[16 * i + 8 * s + b : 16 * i + 8 * s + b + 1, :] = got


def score_some(pos, own, other, toks, exts, picks, where):
    places = [locate(ext, pos) for ext in exts]
    for i, (at_a, at_b) in enumerate(places):
        where[16 * i : 16 * i + 8, :] = at_a
        where[16 * i + 8 : 16 * i + 16, :] = at_b
    tok = toks[0] if len(toks) == 1 else jnp.concatenate(toks, axis=0)
    pick_into(picks, (own, other), tok, places)
    return tok


def score_body(pos, own, other, first, exts, t4, t5, picks, where, rows):
    some = [exts[8 * i : 8 * i + 8, :] for i in range(4)] + [t[R : R + 8, 0:384].astype(F32) for t in (t4, t5)]
    rows[...] = score_some(
        pos, own, other, [first[...]] + [t[0:R, :] for t in (t4, t5)], some, picks, where
    )


def back_body(first, n):
    def body(own, other, where, *refs):
        chunks, (picks, *rows) = refs[:n], refs[n:]
        toks = [c[...] for c in chunks]
        places = []
        for i in range(n):
            at = 16 * (first + i)
            places.append((where[at : at + 8, :], where[at + 8 : at + 16, :]))
        tok = toks[0] if n == 1 else jnp.concatenate(toks, axis=0)
        for out in rows:
            out[...] = tok
        pick_into(picks, (own, other), tok, places)

    return body


def halves_of(packed):
    first = jnp.concatenate([packed[16 * m : 16 * m + 8, :] for m in range(8)], axis=0)
    second = jnp.concatenate([packed[16 * m + 8 : 16 * m + 16, :] for m in range(8)], axis=0)
    return first, second


def squeeze(picks, live, rank):
    first, second = halves_of(picks)
    lane = lanes_iota((64, 128))
    left = jnp.where(live, lane - rank, 0)
    for k in range(7):
        step = 128 - (1 << k)
        left_in = pltpu.roll(left, step, 1)
        hit = ((left_in >> k) & 1) == 1
        first = jnp.where(hit, pltpu.roll(first, step, 1), first)
        second = jnp.where(hit, pltpu.roll(second, step, 1), second)
        left = jnp.where(hit, left_in, jnp.where(((left >> k) & 1) == 1, 0, left))
    lane = lanes_iota((32, 128))
    out = jnp.zeros((32, 128), F32)
    for q, part in enumerate((first[0:32], first[32:64], second[0:32], second[32:64])):
        moved = part if q == 0 else pltpu.roll(part, 32 * q, 1)
        out = jnp.where((lane >> 5) == q, moved, out)
    return out


def unsqueeze(got, rank):
    parts = [got] + [pltpu.roll(got, 128 - 32 * q, 1) for q in (1, 2, 3)]
    first = jnp.concatenate(parts[0:2], axis=0)
    second = jnp.concatenate(parts[2:4], axis=0)
    index = jnp.minimum(rank, CAP - 1)
    out = []
    for m in range(8):
        for half in (first, second):
            out.append(
                jnp.take_along_axis(
                    half[8 * m : 8 * m + 8, :], index[8 * m : 8 * m + 8, :], axis=1, mode="promise_in_bounds"
                )
            )
    return jnp.concatenate(out, axis=0)


def send_body(pos, own, other, t6, t7, p0, w0, gram, out, where, ranks, p1, w1):
    late = (t6, t7)
    score_some(pos, own, other, [t[0:R, :] for t in late], [t[R : R + 8, 0:384].astype(F32) for t in late], p1, w1)
    picks = jnp.concatenate([p0[...], p1[...]], axis=0)
    at = jnp.concatenate([w0[...], w1[...]], axis=0)
    where[...] = at
    live = halves_of(at)[0] >= 0
    before = (rows_iota((128, 128)) < lanes_iota((128, 128))).astype(F32).astype(BF)
    rank = dot(jnp.where(live, 1.0, 0.0).astype(BF), before, NN).astype(I32)
    ranks[...] = rank
    sent = squeeze(picks, live, rank).astype(BF)
    high = gram[...].astype(BF)
    low = (gram[...] - high.astype(F32)).astype(BF)
    for d in range(NY):
        out[d, 0:32, :] = sent
        out[d, 32:48, :] = high[16 * d : 16 * d + 16, :]
        out[d, 48:64, :] = low[16 * d : 16 * d + 16, :]


def resend_body(p0, p1, where, ranks, rows, out):
    picks = jnp.concatenate([p0[...], p1[...]], axis=0)
    live = halves_of(where[...])[0] >= 0
    sent = squeeze(picks, live, ranks[...]).astype(BF)
    for d in range(NY):
        out[d, 0:32, :] = sent
        out[d, 32:64, :] = rows[...]


def total(got, lo, hi):
    acc = got[0, lo:hi, :].astype(F32)
    for d in range(1, NY):
        acc = acc + got[d, lo:hi, :].astype(F32)
    return acc


def table_rows(at_t, val_t, m, half):
    lane = lanes_iota((R, 128))
    parts = []
    for q in range(4):
        k = 16 * m + 4 * half + q
        first = jnp.where(lane == at_t[:, k : k + 1], val_t[:, k : k + 1], 0.0)
        second = jnp.where(lane == at_t[:, k + 8 : k + 9], val_t[:, k + 8 : k + 9], 0.0)
        parts.append((first + second).astype(BF))
    return jnp.concatenate(parts, axis=1)


def decode(at_t, val_t, own, other, ms):
    halves = []
    for half, table in enumerate((own, other)):
        rows = [table_rows(at_t, val_t, m, half) for m in ms]
        rows = rows[0] if len(ms) == 1 else jnp.concatenate(rows, axis=0)
        halves.append(dot(rows, table[0 : 4 * R, :], NN))
    return halves[0] + halves[1]


def act_body(got, own, other, where, ranks, act, at_t, act_t, gram_rows, out7, out5):
    pre = unsqueeze(total(got, 0, 32), ranks[...])
    bias = []
    for table in (own, other):
        for q in range(4):
            ext = table[4 * R + 8 * q : 4 * R + 8 * q + 8, 0:384].astype(F32)
            bias.append((ext[0:1, 0:128] + ext[0:1, 128:256]) + ext[0:1, 256:384])
    bias = jnp.concatenate(bias, axis=0)
    at = where[...]
    shift = [
        jnp.take_along_axis(bias, jnp.maximum(at[8 * k : 8 * k + 8, :], 0), axis=1, mode="promise_in_bounds")
        for k in range(16)
    ]
    pre = pre + jnp.concatenate(shift, axis=0)
    value = jnp.where(at >= 0, pre.astype(BF).astype(F32), 0.0)
    act[...] = value
    turned = at.astype(F32).T.astype(I32)
    value_t = value.T
    at_t[...] = turned
    act_t[...] = value_t
    rows = total(got, 32, 48) + total(got, 48, 64)
    high = rows.astype(BF)
    gram_rows[0:16, :] = high
    gram_rows[16:32, :] = (rows - high.astype(F32)).astype(BF)
    sums = decode(turned, value_t, own, other, (7, 5)).astype(BF)
    out7[...] = sums[:R, :]
    out5[...] = sums[R:, :]


def decode_body(ms):
    def body(at_t, act_t, own, other, *outs):
        got = decode(at_t[...], act_t[...], own, other, ms)
        for i, out in enumerate(outs):
            out[...] = got[i * R : (i + 1) * R, :].astype(out.dtype)

    return body


def turned_table(at, val, b):
    atom = rows_iota((R, 128))
    parts = []
    for m in range(8):
        k = 16 * m + b
        first = jnp.where(atom == at[k : k + 1, :], val[k : k + 1, :], 0.0)
        second = jnp.where(atom == at[k + 8 : k + 9, :], val[k + 8 : k + 9, :], 0.0)
        parts.append(first + second)
    return parts


def load_rows(most, late, rows, sem):
    first = 8 - len(late)
    copies = [pltpu.make_async_copy(most, rows.at[pl.ds(0, first * R)], sem.at[0])]
    for i, ref in enumerate(late):
        to = rows.at[pl.ds((first + i) * R, R)]
        copies.append(pltpu.make_async_copy(ref.at[pl.ds(0, R)], to, sem.at[1 + i]))
    for copy in copies:
        copy.start()
    return copies


def tables_body(c0, c1, c2, c3, t0, t1, t2, t3, enc, dec, rows, exts):
    for i, ref in enumerate((c0, c1, c2, c3)):
        enc[R * i : R * (i + 1), :] = ref[0:R, :]
        dec[R * i : R * (i + 1), :] = ref[R : 2 * R, :]
        dec[4 * R + 8 * i : 4 * R + 8 * i + 8, :] = ref[2 * R : 2 * R + 8, :]
    for i, ref in enumerate((t0, t1, t2, t3)):
        rows[R * i : R * (i + 1), :] = ref[0:R, :]
        exts[8 * i : 8 * i + 8, :] = ref[R : R + 8, 0:384].astype(F32)


def fitted_body(half):
    def body(at, act, after, most, last, out, rows, sem):
        copies = load_rows(most, (last,), rows, sem)
        parts = [jnp.concatenate(turned_table(at, act, 4 * half + q), axis=1).astype(BF) for q in range(4)]
        table = jnp.concatenate(parts, axis=0)
        for copy in copies:
            copy.wait()
        out[...] = (dot(table, rows[...], NN) * LOSS_GRAD).astype(BF)

    return body


def encgrad_body(half):
    def body(got, at, ranks, most, t6, t7, *rest):
        out, (rows, sem) = rest[0], rest[-2:]
        copies = load_rows(most, (t6, t7), rows, sem)
        grad = jnp.where(at[...] >= 0, unsqueeze(total(got, 0, 32), ranks[...]) * LOSS_GRAD, 0.0)
        if half == 0:
            gram = rest[1]
            for d in range(NY):
                gram[16 * d : 16 * d + 16, :] = got[d, 32:48, :].astype(F32) + got[d, 48:64, :].astype(F32)
        parts, ones = [], jnp.ones((8, 128), F32)
        for q in range(4):
            pieces = turned_table(at, grad, 4 * half + q)
            acc = pieces[0]
            for piece in pieces[1:]:
                acc = acc + piece
            sums = lax.dot_general(ones, acc, NT, precision=lax.Precision.HIGHEST, preferred_element_type=F32)
            out[q, R : R + 8, 0:128] = sums.astype(BF)
            out[q, R : R + 8, 128:1024] = jnp.zeros((8, 896), BF)
            parts.append(jnp.concatenate(pieces, axis=1).astype(BF))
        table = jnp.concatenate(parts, axis=0)
        for copy in copies:
            copy.wait()
        part = dot(table, rows[...], NN).astype(BF)
        for q in range(4):
            out[q, 0:R, :] = part[q * R : (q + 1) * R, :]

    return body


def penalty_body(count, gram_ref, decoder, out):
    gram = gram_ref[...]
    row, col = rows_iota((R, R)), lanes_iota((R, R))
    diagonal = row == col
    kept = jnp.where(diagonal, gram, 0.0)
    norm_c = jnp.sqrt(jnp.sum(kept, axis=1, keepdims=True) + EPSILON)
    norm_r = jnp.sqrt(jnp.sum(kept, axis=0, keepdims=True) + EPSILON)
    live = count[0] * BLOCK
    pair = norm_c * norm_r
    cosine = gram / pair
    alive = (row < live) & (col < live) & jnp.logical_not(diagonal)
    coupled = jnp.where(alive, cosine, 0.0)
    spread = jnp.sum(coupled * cosine, axis=1, keepdims=True)
    diag_term = jnp.where(diagonal, spread / (norm_c * norm_c), 0.0)
    weights = (4.0 * COHERENCE * (coupled / pair - diag_term)).astype(BF)
    out[...] = dot(weights, decoder[...], NN)


def finish_body(a, b, c, out, bias):
    total_of = lambda lo, hi, n: a[lo:hi, 0:n].astype(F32) + b[lo:hi, 0:n].astype(F32) + c[lo:hi, 0:n].astype(F32)
    out[...] = total_of(0, R, 1024).astype(BF)
    bias[...] = total_of(R, R + 8, R)


def add(a, b):
    return (a.astype(F32) + b.astype(F32)).astype(BF)


def gather_z(own):
    f1, b1 = move(own, dz=1), move(own, dz=-1)
    f2, b2 = move(f1, dz=1), move(b1, dz=-1)
    f3, b3 = move(f2, dz=1), move(b2, dz=-1)
    return [own, f1, b1, f2, b2, f3, b3, move(f3, dz=1)]


def scatter_x(own, theirs):
    blocks = [add(own[i], theirs[i]) for i in range(4)]
    far = move(blocks[3], dx=1)
    prev = move(blocks[1], dx=-1)
    return blocks[0], prev, move(add(blocks[2], far), dx=1)


def per_device(tokens, dec_bias, encoder, enc_bias, decoder, atom_ids, block_count):
    place = lax.axis_index("atoms")
    pos = jnp.stack([place >> 4, (place >> 1) & 7, place & 1]).astype(I32)
    bias_row = dec_bias.reshape(1, -1)

    sent = call(center_body, sds((R + 8, 1024), BF), tokens, bias_row, atom_ids, specs=whole(3))
    packed, gram_part = call(
        pack_body,
        (sds((2 * R + 8, 1024), BF), sds((R, R), F32)),
        encoder, decoder, enc_bias.reshape(1, -1), sent, specs=whole(3) + [ANY_SPEC],
    )
    tok = gather_z(sent)

    x1, x2 = move(packed, dx=1), move(packed, dx=-1)
    x3 = move(x1, dx=1)
    enc_own, dec_own, tok_first, tok_exts = call(
        tables_body,
        (sds((4 * R, 1024), BF), sds((4 * R + 32, 1024), BF), sds((4 * R, 1024), BF), sds((32, 384), F32)),
        packed, x1, x2, x3, *tok[0:4], specs=whole(8),
    )
    enc_other = move(enc_own, dc=1)
    dec_other = move(dec_own, dc=1)

    pick_most, where_most, tok_most = call(
        score_body, (sds((96, 128), F32), sds((96, 128), I32), sds((6 * R, 1024), BF)),
        pos, enc_own, enc_other, tok_first, tok_exts, *tok[4:6], specs=[SMEM_SPEC] + whole(6),
    )
    out, where, ranks = call(
        send_body, (sds((NY, 64, 128), BF), sds((R, R), I32), sds((64, R), I32)),
        pos, enc_own, enc_other, *tok[6:8], pick_most, where_most, gram_part, specs=[SMEM_SPEC] + whole(7),
        scratch=[pltpu.VMEM((32, 128), F32), pltpu.VMEM((32, 128), I32)],
    )
    got = lax.all_to_all(out, "width", split_axis=0, concat_axis=0, tiled=True)

    act, at_t, act_t, gram_rows, d7, d5 = call(
        act_body,
        (sds((R, R), F32), sds((R, R), I32), sds((R, R), F32), sds((32, 128), BF), sds((R, 1024), BF), sds((R, 1024), BF)),
        got, dec_own, dec_other, where, ranks, specs=whole(5),
    )

    def decoded(ms, last=BF):
        return call(
            decode_body(ms), (sds((R, 1024), BF), sds((R, 1024), last)),
            at_t, act_t, dec_own, dec_other, specs=whole(4),
        )

    d6, d3 = decoded((6, 3))
    d4, d1 = decoded((4, 1))
    d2, d0 = decoded((2, 0), F32)
    f = move(d7, dz=1)
    b = move(d5, dz=-1)
    f = move(add(d6, f), dz=1)
    b = move(add(d3, b), dz=-1)
    f = move(add(d4, f), dz=1)
    b = move(add(d1, b), dz=-1)
    f = move(add(d2, f), dz=1)
    summed = d0 + f.astype(F32) + b.astype(F32)
    residual = (summed + bias_row - tokens.astype(F32)).astype(BF)

    res = gather_z(residual)

    def back(chunks, first):
        n = len(chunks)
        rows = [sds((n * R, 1024), BF)] if n > 1 else []
        return call(
            back_body(first, n), (sds((16 * n, 128), F32), *rows),
            dec_own, dec_other, where, *chunks, specs=whole(3 + n),
        )

    back_most, res_most = back(res[0:7], 0)
    (back_last,) = back(res[7:8], 7)
    out2 = call(resend_body, sds((NY, 64, 128), BF), back_most, back_last, where, ranks, gram_rows, specs=whole(5))
    got2 = lax.all_to_all(out2, "width", split_axis=0, concat_axis=0, tiled=True)

    scratch = [pltpu.VMEM((8 * R, 1024), BF), pltpu.SemaphoreType.DMA((3,))]

    def fitted(half, after):
        return call(
            fitted_body(half), sds((4 * R, 1024), BF), where, act, after, res_most, res[7],
            specs=whole(2) + [ANY_SPEC] * 3, scratch=scratch,
        )

    fit_other = fitted(1, out2)
    fit_theirs = move(fit_other, dc=1)
    fit_own = fitted(0, fit_other)
    fit = scatter_x(fit_own.reshape(4, R, 1024), fit_theirs.reshape(4, R, 1024))

    def encgrad(half):
        outs = [sds((4, R + 8, 1024), BF)] + ([sds((R, R), F32)] if half == 0 else [])
        return call(
            encgrad_body(half), tuple(outs), got2, where, ranks, tok_most, *tok[6:8],
            specs=whole(3) + [ANY_SPEC] * 3, scratch=scratch,
        )

    (eg_other,) = encgrad(1)
    eg_theirs = move(eg_other, dc=1)
    eg_own, gram = encgrad(0)
    eg = scatter_x(eg_own, eg_theirs)
    encoder_grad, bias_grad = call(finish_body, (sds((R, 1024), BF), sds((8, R), F32)), *eg, specs=whole(3))
    bias_grad = bias_grad[0]

    penalty = call(penalty_body, sds((R, 1024), F32), block_count, gram, decoder, specs=[SMEM_SPEC] + whole(2))
    decoder_grad = (fit[0].astype(F32) + fit[1].astype(F32) + fit[2].astype(F32) + penalty).astype(BF)
    return (residual, encoder_grad, decoder_grad, bias_grad)


def solution(mesh):
    in_specs = (
        P("atoms", "width"),
        P("width"),
        P("atoms", "width"),
        P("atoms"),
        P("atoms", "width"),
        P("atoms", None),
        P("atoms"),
    )
    out_specs = (P("atoms", "width"), P("atoms", "width"), P("atoms", "width"), P("atoms"))
    return jax.shard_map(per_device, mesh=mesh, in_specs=in_specs, out_specs=out_specs, check_vma=False)
```
